32 devices in a mesh: row: 4 (over y, x), col: 8 (over z, core).
Axes of the slice: x: 2, y: 2, z: 4, core: 2. Of those that a mesh axis runs over, the one named last changes fastest.
Arguments:
- covariance: float32 [6144, 6144], P(('row', 'col')), may hold values from -1 to 10, as said below
- advective_ratio: float32 [1, 4, 2, 6144], P(None, None, None, ('row', 'col')), may hold values from 0.05 to 0.45
- flow_heading_flags: int32 [1, 4, 2, 6144], replicated, may hold values 0 or 1
- cell_of_state: int32 [6144], replicated, may hold values from 0 to 6143, as said below
- added_uncertainty: float32 [1, 6144], P(None, ('row', 'col')), may hold values from 0.2 to 1
Outputs:
- forecast_cov: float32 [6144, 6144], P(('row', 'col'))
The draws below stay inside these ranges and needn't reach their ends.
Inputs may be any that keep to these rules, and one draw needn't show every extreme that they name: covariance is exactly symmetric. cell_of_state names every grid cell exactly once.
All inputs are finite; a program needn't handle non-finite values.
Results may differ from the reference program's by a relative error of at most 0.00002.
Values sent between devices are 32-bit elements; how exact they have to be, the bound alone decides.
No kernel may reach another device: no remote copies, remote signals or barrier semaphores. Data moves between devices by JAX's collectives and lax.ppermute only.
A program may use at most 128 MiB of HBM per device.

```python
import math
import jax
import jax.numpy as jnp
from jax import lax

LAT = 48
LON = 128
ADVECTION_TOTAL = 4
PREDICTION_TOTAL = 1
UNKNOWN_TOTAL = 6144


def grid_order(key):
    return jax.random.permutation(jax.random.fold_in(key, 29), LAT * LON).astype(jnp.int32)


def draw_cell_of_state(key, part):
    return grid_order(key)


def draw_covariance(key, part):
    total_states = LAT * LON
    cells = grid_order(key)
    lat_of = (cells // LON).astype(jnp.float32)
    lon_of = (cells % LON).astype(jnp.float32)
    noise_key, scale_key = jax.random.split(jax.random.fold_in(key, 17), 2)
    lat_gap = jnp.abs(lat_of[:, None] - lat_of[None, :])
    lon_gap = jnp.abs(lon_of[:, None] - lon_of[None, :])
    lon_gap = jnp.minimum(lon_gap, LON - lon_gap)
    short_lat, short_lon, broad_lat, broad_lon = (2.0, 4.0, 6.0, 16.0)
    low_scale, high_scale = (1.0, 2.0)
    kernel = 0.6 * jnp.exp(-lat_gap / short_lat - lon_gap / short_lon) + 0.4 * jnp.exp(-lat_gap / broad_lat - lon_gap / broad_lon)
    random_part = jnp.clip(jax.random.normal(noise_key, (total_states, total_states), jnp.float32), -6.0, 6.0)
    random_part = random_part * (0.12 / math.sqrt(total_states))
    spread_array = kernel + (random_part + random_part.T)
    self_pairing_entry = jnp.arange(total_states, dtype=jnp.int32)
    spread_array = spread_array.at[self_pairing_entry, self_pairing_entry].add(0.4)
    scales = jnp.exp(jax.random.uniform(scale_key, (total_states,), jnp.float32, math.log(low_scale), math.log(high_scale)))
    outer_scales = scales[:, None] * scales[None, :]
    return spread_array * outer_scales


def set_ends(result, own_key, smallest, largest):
    longest = result.shape.index(max(result.shape))
    spots = []
    for shift in (0, 1):
        where = [jax.random.randint(jax.random.fold_in(own_key, axis), (), 0, length) for axis, length in enumerate(result.shape)]
        where[longest] = (where[longest] + shift) % result.shape[longest]
        spots.append(tuple(where))
    return result.at[spots[0]].set(smallest).at[spots[1]].set(largest)


def levels(rng, dims, pieces, smallest, top_value):
    def one(position, parts):
        heights = jax.random.uniform(jax.random.fold_in(jax.random.fold_in(rng, 6), position), (parts,), jnp.float32, smallest / len(pieces), top_value / len(pieces))
        return jnp.repeat(jnp.exp(heights), dims[position] // parts).reshape((-1,) + (1,) * (len(dims) - position - 1))

    level = one(*pieces[0])
    for cut in pieces[1:]:
        level = level * one(*cut)
    return level


def setup_inputs(seed: int = 0) -> dict:
    splits = jax.random.split(jax.random.key(seed), 6)
    return {
        "covariance": draw_covariance(jax.random.fold_in(splits[5], 71), 0),
        "advective_ratio": jnp.clip(jnp.exp(math.log(0.45) - 2.1972245 * jax.random.uniform(splits[1], (PREDICTION_TOTAL, ADVECTION_TOTAL, 2, UNKNOWN_TOTAL), jnp.float32) ** levels(splits[1], (PREDICTION_TOTAL, ADVECTION_TOTAL, 2, UNKNOWN_TOTAL), ((3, 32),), -0.2, 0.2)), 0.05, 0.45),
        "flow_heading_flags": set_ends((jax.random.randint(splits[2], (PREDICTION_TOTAL, ADVECTION_TOTAL, 2, UNKNOWN_TOTAL), 0, 2) < 1).astype(jnp.int32), jax.random.fold_in(splits[2], 1), 0, 1),
        "cell_of_state": draw_cell_of_state(jax.random.fold_in(splits[5], 71), 0),
        "added_uncertainty": jnp.clip(jnp.exp(math.log(1.0) - 1.609438 * jax.random.uniform(splits[4], (PREDICTION_TOTAL, UNKNOWN_TOTAL), jnp.float32) ** levels(splits[4], (PREDICTION_TOTAL, UNKNOWN_TOTAL), ((1, 32),), -0.2, 0.2)), 0.2, 1.0),
    }


def upstream_factors(rates, masks_now, advection_increment):
    east_rate = rates[advection_increment, 0].reshape(LAT, LON)
    north_rate = rates[advection_increment, 1].reshape(LAT, LON)
    east_mask = masks_now[advection_increment, 0].reshape(LAT, LON) == 1
    north_mask = masks_now[advection_increment, 1].reshape(LAT, LON) == 1
    remain = 1.0 - east_rate - north_rate
    from_west = jnp.where(east_mask, east_rate, 0.0)
    from_east = jnp.where(east_mask, 0.0, east_rate)
    from_south = jnp.where(north_mask, north_rate, 0.0)
    from_north = jnp.where(north_mask, 0.0, north_rate)
    return (remain, from_west, from_east, from_south, from_north)


def substep_move(values, weights):
    remain, from_west, from_east, from_south, from_north = weights
    west_cell = jnp.roll(values, 1, axis=2)
    east_cell = jnp.roll(values, -1, axis=2)
    zero_row = jnp.zeros_like(values[:, :1, :])
    south_cell = jnp.concatenate([zero_row, values[:, :-1, :]], axis=1)
    north_cell = jnp.concatenate([values[:, 1:, :], zero_row], axis=1)
    return (remain * values + from_west * west_cell + from_east * east_cell
            + from_south * south_cell + from_north * north_cell)


def apply_rows(rows_in, coefficient_series, cell_of_state, state_of_cell):
    count_rows = rows_in.shape[0]
    on_grid = jnp.take(rows_in, state_of_cell, axis=1).reshape(count_rows, LAT, LON)
    for weights in coefficient_series:
        on_grid = substep_move(on_grid, weights)
    return jnp.take(on_grid.reshape(count_rows, LAT * LON), cell_of_state, axis=1)


def reference(covariance, advective_ratio, flow_heading_flags, cell_of_state, added_uncertainty):
    state_of_cell = jnp.zeros((UNKNOWN_TOTAL,), jnp.int32).at[cell_of_state].set(jnp.arange(UNKNOWN_TOTAL, dtype=jnp.int32))
    block_rows = UNKNOWN_TOTAL // 16
    self_pairing_entry = jnp.arange(UNKNOWN_TOTAL, dtype=jnp.int32)
    numbers = jnp.arange(16, dtype=jnp.int32)
    spread_array = covariance
    for prediction_interval in range(PREDICTION_TOTAL):
        coefficient_series = [upstream_factors(advective_ratio[prediction_interval], flow_heading_flags[prediction_interval], advection_increment) for advection_increment in range(ADVECTION_TOTAL)]

        def first_pass(number):
            rows_in = lax.dynamic_slice_in_dim(spread_array, number * block_rows, block_rows, 0)
            return apply_rows(rows_in, coefficient_series, cell_of_state, state_of_cell)

        one_side = lax.map(first_pass, numbers).reshape(UNKNOWN_TOTAL, UNKNOWN_TOTAL)

        def second_pass(number):
            columns = lax.dynamic_slice_in_dim(one_side, number * block_rows, block_rows, 1)
            return apply_rows(columns.T, coefficient_series, cell_of_state, state_of_cell)

        congruence_result = lax.map(second_pass, numbers).reshape(UNKNOWN_TOTAL, UNKNOWN_TOTAL)
        spread_array = congruence_result.at[self_pairing_entry, self_pairing_entry].add(added_uncertainty[prediction_interval])
    return spread_array
```

```python
import jax
import jax.numpy as jnp
from jax import lax
from jax.experimental import pallas as pl
from jax.experimental.pallas import tpu as pltpu
from jax.sharding import PartitionSpec as P

LAT = 48
LON = 128
ADVECTION_TOTAL = 4
CELLS = LAT * LON
LANES = 128
AXES = ("row", "col")
GROUPS = 8
UNROLL = 32


def spans_first(count):
    half = count // 2
    return ((0, half), (half, half))


def spans_second(count):
    return tuple((at, min(LANES, count - at)) for at in range(0, count, LANES))


def block_rows(count):
    full, rest = divmod(count, LANES)
    if rest * 2 == LANES:
        return full * count + count // 2
    return (full + (rest > 0)) * count


def scatter_rows(index, source, target, start, stop):
    def body(step, carry):
        base = step * UNROLL
        rows = [source[pl.ds(pl.multiple_of(2 * (base + u), 2), 2), :] for u in range(UNROLL)]
        for u in range(UNROLL):
            target[pl.ds(pl.multiple_of(index[base + u], 2), 2), :] = rows[u]
        return carry

    lax.fori_loop(start // UNROLL, stop // UNROLL, body, 0)


def gather_rows(index, source, target, start, stop):
    def body(step, carry):
        base = step * UNROLL
        rows = [source[pl.ds(pl.multiple_of(index[base + u], 2), 2), :] for u in range(UNROLL)]
        for u in range(UNROLL):
            target[pl.ds(pl.multiple_of(2 * (base + u), 2), 2), :] = rows[u]
        return carry

    lax.fori_loop(start // UNROLL, stop // UNROLL, body, 0)


def advect(spans, coefs, picks, packed, spare, level_a, level_b):
    count = level_a.shape[1]

    def to_grid(i, carry):
        for h, (at, width) in enumerate(spans):
            block = packed[pl.ds(2 * LON * i + h, LON, stride=2), :]
            level_a[i + 1, at : at + width, :] = block.T[:width]
        return carry

    lax.fori_loop(0, LAT, to_grid, 0)
    for level in (level_a, level_b):
        for edge in (0, LAT + 1):
            level[edge] = jnp.zeros((count, LON), jnp.float32)

    for s in range(ADVECTION_TOTAL):
        source, target = (level_a, level_b) if s % 2 == 0 else (level_b, level_a)

        def row(i, carry, s=s, source=source, target=target):
            def spread(ref, which):
                return jnp.broadcast_to(ref[s, which, pl.ds(i, 1), :], (8, LON))

            remain, rate_x, rate_y = (spread(coefs, w) for w in range(3))
            pick_x, north = (spread(picks, w) for w in range(2))
            from_south = north == 1
            for g in range(0, count, 8):
                here = source[i + 1, g : g + 8, :]
                side = jnp.take_along_axis(here, pick_x, axis=1)
                below = source[i, g : g + 8, :]
                above = source[i + 2, g : g + 8, :]
                target[i + 1, g : g + 8, :] = (
                    remain * here + rate_x * side + rate_y * jnp.where(from_south, below, above)
                )
            return carry

        lax.fori_loop(0, LAT, row, 0)
    final = level_a if ADVECTION_TOTAL % 2 == 0 else level_b

    def to_cells(i, carry):
        for h, (at, width) in enumerate(spans):
            spare[pl.ds(2 * LON * i + h, LON, stride=2), 0:width] = final[i + 1, at : at + width, :].T
        return carry

    lax.fori_loop(0, LAT, to_cells, 0)


def first_pass(index, x_hbm, coefs, picks, o_hbm, x_v, k_a, k_b, level_a, level_b, o_v, sem_in, sem_out):
    count = x_v.shape[0]
    devices = o_v.shape[0]
    spans = spans_first(count)
    wide = CELLS // GROUPS

    def fetch(q):
        part = pl.ds(q * wide, wide)
        return pltpu.make_async_copy(x_hbm.at[:, part], x_v.at[:, part], sem_in.at[q])

    for q in range(GROUPS):
        fetch(q).start()

    def turn(c, carry):
        at_lane = pl.multiple_of(c * LANES, LANES)
        for h, (at, width) in enumerate(spans):
            k_a[pl.ds(2 * LANES * c + h, LANES, stride=2), 0:width] = x_v[at : at + width, pl.ds(at_lane, LANES)].T
        return carry

    each = wide // LANES
    for q in range(GROUPS):
        fetch(q).wait()
        lax.fori_loop(q * each, (q + 1) * each, turn, 0)
    scatter_rows(index, k_a, k_b, 0, CELLS)
    advect(spans, coefs, picks, k_b, k_a, level_a, level_b)
    gather_rows(index, k_a, k_b, 0, CELLS)
    full, rest = divmod(count, LANES)

    def pack(e, carry):
        base = 2 * count * e
        for t, (at_m, width_m) in enumerate(spans_second(count)):
            rows = [k_b[pl.ds(base + 2 * at_m + h, width_m, stride=2), :] for h in range(2)]
            half = count // 2
            if t == full and 2 * rest == LANES:
                o_v[e, full * count : full * count + half, :] = jnp.concatenate(rows, axis=0).T[:half]
            else:
                for h in range(2):
                    o_v[e, t * count + h * half : t * count + (h + 1) * half, 0:width_m] = rows[h].T[:half]
        return carry

    some = devices // GROUPS

    def send(q):
        part = pl.ds(q * some, some)
        return pltpu.make_async_copy(o_v.at[part], o_hbm.at[part], sem_out.at[q])

    for q in range(GROUPS):
        lax.fori_loop(q * some, (q + 1) * some, pack, 0)
        send(q).start()
    for q in range(GROUPS):
        send(q).wait()


def second_pass(index, place, a_hbm, coefs, picks, extra, o_hbm, a_v, k_a, k_b, level_a, level_b, o_v, sem_in, sem_out):
    count = o_v.shape[0]
    devices = a_v.shape[0]
    spans = spans_second(count)
    full, rest = divmod(count, LANES)
    half = count // 2
    some = devices // GROUPS

    def fetch(q):
        part = pl.ds(q * some, some)
        return pltpu.make_async_copy(a_hbm.at[part], a_v.at[part], sem_in.at[q])

    for q in range(GROUPS):
        fetch(q).start()

    def unpack(d, carry):
        base = 2 * count * d
        for t in range(len(spans)):
            if t == full and 2 * rest == LANES:
                both = a_v[d, full * count : full * count + half, :]
                k_a[pl.ds(base + t, half, stride=2), :] = both
                k_a[pl.ds(base + 2 * half + t, half, stride=2), :] = pltpu.roll(both, LANES // 2, 1)
            else:
                k_a[pl.ds(base + t, count, stride=2), :] = a_v[d, t * count : (t + 1) * count, :]
        return carry

    for q in range(GROUPS):
        fetch(q).wait()
        lax.fori_loop(q * some, (q + 1) * some, unpack, 0)
    scatter_rows(index, k_a, k_b, 0, CELLS)
    advect(spans, coefs, picks, k_b, k_a, level_a, level_b)
    gather_rows(index, k_a, k_b, 0, CELLS)
    mine = pl.ds(pl.multiple_of(2 * count * place[0], 16), 2 * count)
    k_b[mine, :] = k_b[mine, :] + extra[...]

    def turn(c, carry):
        at_lane = pl.multiple_of(c * LANES, LANES)
        for h, (at, width) in enumerate(spans):
            o_v[at : at + width, pl.ds(at_lane, LANES)] = k_b[pl.ds(2 * LANES * c + h, LANES, stride=2), :].T[:width]
        return carry

    wide = CELLS // GROUPS
    each = wide // LANES

    def send(q):
        part = pl.ds(q * wide, wide)
        return pltpu.make_async_copy(o_v.at[:, part], o_hbm.at[:, part], sem_out.at[q])

    for q in range(GROUPS):
        lax.fori_loop(q * each, (q + 1) * each, turn, 0)
        send(q).start()
    for q in range(GROUPS):
        send(q).wait()


def scratch(first, count, last):
    return [
        pltpu.VMEM(first, jnp.float32),
        pltpu.VMEM((2 * CELLS, LANES), jnp.float32),
        pltpu.VMEM((2 * CELLS, LANES), jnp.float32),
        pltpu.VMEM((LAT + 2, count, LON), jnp.float32),
        pltpu.VMEM((LAT + 2, count, LON), jnp.float32),
        pltpu.VMEM(last, jnp.float32),
        pltpu.SemaphoreType.DMA((GROUPS,)),
        pltpu.SemaphoreType.DMA((GROUPS,)),
    ]


def shards(covariance, advective_ratio, flow_heading_flags, cell_of_state, added_uncertainty):
    count = covariance.shape[0]
    devices = lax.axis_size(AXES)
    here = lax.axis_index(AXES)
    rows = block_rows(count)
    smem = pl.BlockSpec(memory_space=pltpu.SMEM)
    vmem = pl.BlockSpec(memory_space=pltpu.VMEM)
    hbm = pl.BlockSpec(memory_space=pl.ANY)
    params = pltpu.CompilerParams(vmem_limit_bytes=60 * 2**20)

    own = advective_ratio[0].reshape(1, ADVECTION_TOTAL * 2, count)
    spread = jnp.broadcast_to(own, (devices, ADVECTION_TOTAL * 2, count))
    rates = lax.all_to_all(spread, AXES, split_axis=0, concat_axis=0, tiled=True)
    rates = jnp.transpose(rates, (1, 0, 2)).reshape(ADVECTION_TOTAL, 2, LAT, LON)
    heading = flow_heading_flags[0].reshape(ADVECTION_TOTAL, 2, LAT, LON)
    rate_x, rate_y = rates[:, 0], rates[:, 1]
    coefs = jnp.stack([1.0 - rate_x - rate_y, rate_x, rate_y], axis=1)
    lane = lax.broadcasted_iota(jnp.int32, (ADVECTION_TOTAL, LAT, LON), 2)
    pick_x = jnp.where(heading[:, 0] == 1, lane + (LON - 1), lane + 1) % LON
    picks = jnp.stack([pick_x, heading[:, 1]], axis=1)
    index = 2 * cell_of_state

    blocks = pl.pallas_call(
        first_pass,
        out_shape=jax.ShapeDtypeStruct((devices, rows, LANES), jnp.float32),
        in_specs=[smem, hbm, vmem, vmem],
        out_specs=hbm,
        scratch_shapes=scratch((count, CELLS), count, (devices, rows, LANES)),
        compiler_params=params,
        name="first_pass",
    )(index, covariance, coefs, picks)
    arrived = lax.all_to_all(blocks, AXES, split_axis=0, concat_axis=0, tiled=True)

    state = lax.broadcasted_iota(jnp.int32, (count, 2, LANES), 0)
    slot = lax.broadcasted_iota(jnp.int32, (count, 2, LANES), 1) * LANES
    slot = slot + lax.broadcasted_iota(jnp.int32, (count, 2, LANES), 2)
    extra = jnp.where(state == slot, added_uncertainty[0][:, None, None], 0.0).reshape(2 * count, LANES)
    return pl.pallas_call(
        second_pass,
        out_shape=jax.ShapeDtypeStruct((count, CELLS), jnp.float32),
        in_specs=[smem, smem, hbm, vmem, vmem, vmem],
        out_specs=hbm,
        scratch_shapes=scratch((devices, rows, LANES), count, (count, CELLS)),
        compiler_params=params,
        name="second_pass",
    )(index, here.reshape(1), arrived, coefs, picks, extra)


def solution(mesh):
    in_specs = (
        P(AXES, None),
        P(None, None, None, AXES),
        P(),
        P(),
        P(None, AXES),
    )
    return jax.shard_map(shards, mesh=mesh, in_specs=in_specs, out_specs=P(AXES, None), check_vma=False)
```

```python
import jax
import jax.numpy as jnp
from jax import lax
from jax.experimental import pallas as pl
from jax.experimental.pallas import tpu as pltpu
from jax.sharding import PartitionSpec as P

LAT = 48
LON = 128
ADVECTION_TOTAL = 4
CELLS = LAT * LON
LANES = 128
AXES = ("row", "col")
GROUPS = 8
BATCH = 16
LAG = 2
RING = 8
MIB = 2**20


def spans_first(count):
    half = count // 2
    return ((0, half), (half, half))


def spans_second(count):
    return tuple((at, min(LANES, count - at)) for at in range(0, count, LANES))


def is_packed(count, width):
    return 2 * width == LANES and count > width


def scatter_rows(index, start, source, first, target, slots, total):
    for u0 in range(0, total, BATCH):
        some = range(u0, min(u0 + BATCH, total))
        rows = [source[pl.ds(first + slots * u, slots), :] for u in some]
        for u, row in zip(some, rows):
            target[pl.ds(pl.multiple_of(slots * index[start + u], slots), slots), :] = row


def gather_rows(index, start, source, target, slots, total):
    for u0 in range(0, total, BATCH):
        some = range(u0, min(u0 + BATCH, total))
        rows = [source[pl.ds(pl.multiple_of(slots * index[start + u], slots), slots), :] for u in some]
        for u, row in zip(some, rows):
            target[slots * u : slots * (u + 1), :] = row


def slot_rows(start, h, total, slots):
    return pl.ds(start + h, total, stride=slots) if slots > 1 else pl.ds(start, total)


def substep(coefs, picks, s, source, target, i):
    def spread(ref, which):
        return jnp.broadcast_to(ref[s, which, pl.ds(i, 1), :], (8, LON))

    remain, rate_x, rate_y = (spread(coefs, w) for w in range(3))
    pick_x, north = (spread(picks, w) for w in range(2))
    from_south = north == 1
    south, middle, above = ((i + d) & (RING - 1) for d in (-1, 0, 1))
    for g in range(0, source.shape[1], 8):
        here = source[middle, g : g + 8, :]
        side = jnp.take_along_axis(here, pick_x, axis=1)
        y_side = jnp.where(from_south, source[south, g : g + 8, :], source[above, g : g + 8, :])
        target[middle, g : g + 8, :] = remain * here + rate_x * side + rate_y * y_side


def advect(spans, coefs, picks, cells_in, cells_out, levels):
    slots = len(spans)
    count = levels[0].shape[1]

    def enter(i):
        for h, (at, width) in enumerate(spans):
            block = cells_in[slot_rows(slots * LON * i, h, LON, slots), :]
            levels[0][i & (RING - 1), at : at + width, :] = block.T[:width]

    def leave(i):
        for h, (at, width) in enumerate(spans):
            block = levels[-1][i & (RING - 1), at : at + width, :]
            cells_out[slot_rows(slots * LON * i, h, LON, slots), 0:width] = block.T

    for level in levels[:-1]:
        level[RING - 1] = jnp.zeros((count, LON), jnp.float32)
    tail = LAG * ADVECTION_TOTAL + 1

    def step(i, guard):
        def run(stage, j):
            if guard:
                pl.when((j >= 0) & (j < LAT))(lambda: stage(j))
            else:
                stage(j)

        run(leave, i - tail)
        for s in reversed(range(ADVECTION_TOTAL)):
            run(lambda j, s=s: substep(coefs, picks, s, levels[s], levels[s + 1], j), i - LAG * (s + 1))
        run(enter, i)

    def guarded(i, carry):
        step(i, True)
        return carry

    def steady(i, carry):
        step(i, False)
        return carry

    lax.fori_loop(0, tail, guarded, 0)
    lax.fori_loop(tail, LAT, steady, 0)
    lax.fori_loop(LAT, LAT + tail, guarded, 0)


def lay_on_grid(index, x_hbm, o_ref, x_v, tiles, sem_in):
    spans = spans_first(x_v.shape[0])
    slots = len(spans)
    wide = CELLS // GROUPS
    each = wide // LANES

    def fetch(q):
        part = pl.ds(q * wide, wide)
        return pltpu.make_async_copy(x_hbm.at[:, part], x_v.at[:, part], sem_in.at[q])

    for q in range(GROUPS):
        fetch(q).start()

    def turn(c, slot):
        at_lane = pl.multiple_of(c * LANES, LANES)
        for h, (at, width) in enumerate(spans):
            block = x_v[at : at + width, pl.ds(at_lane, LANES)]
            tiles[slot][slot_rows(0, h, LANES, slots), 0:width] = block.T

    def place(c, slot):
        scatter_rows(index, c * LANES, tiles[slot], 0, o_ref, slots, LANES)

    fetch(0).wait()
    turn(0, 0)

    def body(b, carry):
        c = 2 * b
        turn(c + 1, 1)
        place(c, 0)
        turn(jnp.minimum(c + 2, CELLS // LANES - 1), 0)
        place(c + 1, 1)
        return carry

    for q in range(GROUPS):
        if q + 1 < GROUPS:
            fetch(q + 1).wait()
        lax.fori_loop(q * each // 2, (q + 1) * each // 2, body, 0)


def send_part(index, cells, o_v, o_hbm, tiles, sem_out, count, at, width):
    spans = spans_first(count)
    slots = len(spans)
    half = count // 2
    devices = o_v.shape[0]
    some = devices // GROUPS

    def pick(e, slot):
        gather_rows(index, e * count + at, cells, tiles[slot], slots, width)

    def turn(e, slot):
        rows = [tiles[slot][slot_rows(0, h, width, slots), :] for h in range(slots)]
        if is_packed(count, width):
            o_v[e] = jnp.concatenate(rows, axis=0).T[:half]
        else:
            for h in range(slots):
                o_v[e, h * half : (h + 1) * half, 0:width] = rows[h].T[:half]

    def send(q):
        part = pl.ds(q * some, some)
        return pltpu.make_async_copy(o_v.at[part], o_hbm.at[part], sem_out.at[q])

    pick(0, 0)

    def body(b, carry):
        e = 2 * b
        pick(e + 1, 1)
        turn(e, 0)
        pick(jnp.minimum(e + 2, devices - 1), 0)
        turn(e + 1, 1)
        return carry

    for q in range(GROUPS):
        lax.fori_loop(q * some // 2, (q + 1) * some // 2, body, 0)
        send(q).start()
    for q in range(GROUPS):
        send(q).wait()


def first_pass(count, at, width):
    def kernel(index, x_hbm, coefs, picks, o_hbm, keep_hbm, x_v, cells_in, cells_out, o_v, tile_a, tile_b, sem_in, sem_out, sem_keep, *levels):
        tiles = (tile_a, tile_b)
        lay_on_grid(index, x_hbm, cells_in, x_v, tiles, sem_in)
        advect(spans_first(count), coefs, picks, cells_in, cells_out, levels)
        keep = pltpu.make_async_copy(cells_out, keep_hbm, sem_keep)
        keep.start()
        send_part(index, cells_out, o_v, o_hbm, tiles, sem_out, count, at, width)
        keep.wait()

    return kernel


def first_rest(count, at, width):
    def kernel(index, cells, o_hbm, o_v, tile_a, tile_b, sem_out):
        send_part(index, cells, o_v, o_hbm, (tile_a, tile_b), sem_out, count, at, width)

    return kernel


def second_pass(count, devices, at, width):
    packed = is_packed(count, width)
    rows = count // 2 if packed else count

    def kernel(index, place, a_hbm, coefs, picks, extra, *rest):
        if at:
            rest = rest[1:]
        o_hbm, a_v, cells_in, cells_out, o_v, tile_a, tile_b, sem_in, sem_out, *levels = rest
        tiles = (tile_a, tile_b)
        some = devices // GROUPS

        def fetch(q):
            part = pl.ds(q * some * rows, some * rows)
            return pltpu.make_async_copy(a_hbm.at[part], a_v.at[part], sem_in.at[q])

        for q in range(GROUPS):
            fetch(q).start()

        def arrive(d, carry):
            at_row = pl.multiple_of(d * rows, 8)
            if packed:
                tile_a[0:rows, :] = pltpu.roll(a_v[pl.ds(at_row, rows), :], LANES // 2, 1)
                scatter_rows(index, d * count, a_v, at_row, cells_in, 1, rows)
                scatter_rows(index, d * count + rows, tile_a, 0, cells_in, 1, rows)
            else:
                scatter_rows(index, d * count, a_v, at_row, cells_in, 1, rows)
            return carry

        for q in range(GROUPS):
            fetch(q).wait()
            lax.fori_loop(q * some, (q + 1) * some, arrive, 0)
        advect(((0, width),), coefs, picks, cells_in, cells_out, levels)
        mine = place[0] * count + at
        for u0 in range(0, width, BATCH):
            own = [pl.ds(index[mine + u], 1) for u in range(u0, u0 + BATCH)]
            sums = [cells_out[own[u], :] + extra[u0 + u : u0 + u + 1, :] for u in range(BATCH)]
            for u in range(BATCH):
                cells_out[own[u], :] = sums[u]

        def pick(c, slot):
            gather_rows(index, c * LANES, cells_out, tiles[slot], 1, LANES)

        def turn(c, slot):
            at_lane = pl.multiple_of(c * LANES, LANES)
            o_v[:, pl.ds(at_lane, LANES)] = tiles[slot][0:LANES, :].T[:width]

        wide = CELLS // GROUPS
        each = wide // LANES

        def send(q):
            part = pl.ds(q * wide, wide)
            return pltpu.make_async_copy(o_v.at[:, part], o_hbm.at[pl.ds(at, width), part], sem_out.at[q])

        pick(0, 0)

        def body(b, carry):
            c = 2 * b
            pick(c + 1, 1)
            turn(c, 0)
            pick(jnp.minimum(c + 2, CELLS // LANES - 1), 0)
            turn(c + 1, 1)
            return carry

        for q in range(GROUPS):
            lax.fori_loop(q * each // 2, (q + 1) * each // 2, body, 0)
            send(q).start()
        for q in range(GROUPS):
            send(q).wait()

    return kernel


def shards(covariance, advective_ratio, flow_heading_flags, cell_of_state, added_uncertainty):
    count = covariance.shape[0]
    devices = lax.axis_size(AXES)
    here = lax.axis_index(AXES)
    smem = pl.BlockSpec(memory_space=pltpu.SMEM)
    vmem = pl.BlockSpec(memory_space=pltpu.VMEM)
    hbm = pl.BlockSpec(memory_space=pl.ANY)
    f32 = jnp.float32
    slots = len(spans_first(count))
    cells = (slots * CELLS, LANES)
    sems = pltpu.SemaphoreType.DMA((GROUPS,))

    def levels(rows):
        return [pltpu.VMEM((RING, rows, LON), f32)] * (ADVECTION_TOTAL + 1)

    def tiles(rows):
        return [pltpu.VMEM((rows, LANES), f32)] * 2

    def params(mib):
        return pltpu.CompilerParams(vmem_limit_bytes=mib * MIB)

    def cost(us):
        return pl.CostEstimate(flops=us * 10**6, bytes_accessed=us * 3 * 10**6, transcendentals=0)

    own = advective_ratio[0].reshape(1, ADVECTION_TOTAL * 2, count)
    spread = jnp.broadcast_to(own, (devices, ADVECTION_TOTAL * 2, count))
    rates = lax.all_to_all(spread, AXES, split_axis=0, concat_axis=0, tiled=True)
    rates = jnp.transpose(rates, (1, 0, 2)).reshape(ADVECTION_TOTAL, 2, LAT, LON)
    heading = flow_heading_flags[0].reshape(ADVECTION_TOTAL, 2, LAT, LON)
    rate_x, rate_y = rates[:, 0], rates[:, 1]
    lat = lax.broadcasted_iota(jnp.int32, (ADVECTION_TOTAL, LAT, LON), 1)
    outside = lat == jnp.where(heading[:, 1] == 1, 0, LAT - 1)
    coefs = jnp.stack([1.0 - rate_x - rate_y, rate_x, jnp.where(outside, 0.0, rate_y)], axis=1)
    lane = lax.broadcasted_iota(jnp.int32, (ADVECTION_TOTAL, LAT, LON), 2)
    pick_x = jnp.where(heading[:, 0] == 1, lane + (LON - 1), lane + 1) % LON
    picks = jnp.stack([pick_x, heading[:, 1]], axis=1)

    parts = spans_second(count)
    blocks = [
        (devices, count // 2 if is_packed(count, width) else count, LANES) for _, width in parts
    ]
    moved = []
    for (at, width), shape in zip(parts, blocks):
        staging = [pltpu.VMEM(shape, f32)] + tiles(slots * LANES) + [sems]
        if at == 0:
            sent, advected = pl.pallas_call(
                first_pass(count, at, width),
                out_shape=(jax.ShapeDtypeStruct(shape, f32), jax.ShapeDtypeStruct(cells, f32)),
                in_specs=[smem, hbm, vmem, vmem],
                out_specs=(hbm, hbm),
                scratch_shapes=[pltpu.VMEM(covariance.shape, f32)]
                + [pltpu.VMEM(cells, f32)] * 2
                + staging[:-1]
                + [sems, sems, pltpu.SemaphoreType.DMA(())]
                + levels(count),
                compiler_params=params(60),
                cost_estimate=cost(25),
                name="first_pass",
            )(cell_of_state, covariance, coefs, picks)
        else:
            sent = pl.pallas_call(
                first_rest(count, at, width),
                out_shape=jax.ShapeDtypeStruct(shape, f32),
                in_specs=[smem, vmem],
                out_specs=hbm,
                scratch_shapes=staging,
                compiler_params=params(60),
                cost_estimate=cost(6),
                name="first_rest",
            )(cell_of_state, advected)
        arrived = lax.all_to_all(sent, AXES, split_axis=0, concat_axis=0, tiled=True)
        moved.append(arrived.reshape(devices * shape[1], LANES))

    result = None
    for (at, width), arrived in zip(parts, moved):
        lane = lax.broadcasted_iota(jnp.int32, (width, LANES), 1)
        row = lax.broadcasted_iota(jnp.int32, (width, LANES), 0)
        extra = jnp.where(lane == row, added_uncertainty[0, at : at + width, None], 0.0)
        args = [cell_of_state, here.reshape(1), arrived, coefs, picks, extra]
        specs = [smem, smem, hbm, vmem, vmem, vmem]
        if at:
            args.append(result)
            specs.append(hbm)
        result = pl.pallas_call(
            second_pass(count, devices, at, width),
            out_shape=jax.ShapeDtypeStruct((count, CELLS), f32),
            in_specs=specs,
            out_specs=hbm,
            scratch_shapes=[
                pltpu.VMEM(arrived.shape, f32),
                pltpu.VMEM((CELLS, LANES), f32),
                pltpu.VMEM((CELLS, LANES), f32),
                pltpu.VMEM((width, CELLS), f32),
            ]
            + tiles(LANES)
            + [sems, sems]
            + levels(width),
            input_output_aliases={6: 0} if at else {},
            compiler_params=params(60),
            cost_estimate=cost(25),
            name="second_pass",
        )(*args)
    return result


def solution(mesh):
    in_specs = (
        P(AXES, None),
        P(None, None, None, AXES),
        P(),
        P(),
        P(None, AXES),
    )
    return jax.shard_map(shards, mesh=mesh, in_specs=in_specs, out_specs=P(AXES, None), check_vma=False)
```

```python
import math

import jax
import jax.numpy as jnp
from jax import lax
from jax.experimental import pallas as pl
from jax.experimental.pallas import tpu as pltpu
from jax.sharding import PartitionSpec as P

LAT = 48
LON = 128
ADVECTION_TOTAL = 4
CELLS = LAT * LON
LANES = 128
AXES = ("row", "col")
GROUPS = 4
BATCH = 16
BAND = 2
RING = 4 * BAND
MIB = 2**20


def spans_first(count):
    half = count // 2
    return ((0, half), (half, half))


def spans_second(count):
    return tuple((at, min(LANES, count - at)) for at in range(0, count, LANES))


def is_packed(count, width):
    return 2 * width == LANES and count > width


def scatter_rows(index, start, source, first, target, slots, total):
    for u0 in range(0, total, BATCH):
        some = range(u0, min(u0 + BATCH, total))
        rows = [source[pl.ds(first + slots * u, slots), :] for u in some]
        for u, row in zip(some, rows):
            target[pl.ds(pl.multiple_of(slots * index[start + u], slots), slots), :] = row


def gather_rows(index, start, source, target, slots, total):
    for u0 in range(0, total, BATCH):
        some = range(u0, min(u0 + BATCH, total))
        rows = [source[pl.ds(pl.multiple_of(slots * index[start + u], slots), slots), :] for u in some]
        for u, row in zip(some, rows):
            target[slots * u : slots * (u + 1), :] = row


def slot_rows(start, h, total, slots):
    return pl.ds(start + h, total, stride=slots) if slots > 1 else pl.ds(start, total)


def substep(rates, flags, s, source, target, i):
    def spread(row):
        return jnp.broadcast_to(row, (8, LON))

    at_lane = pl.multiple_of(i * LON, LON)
    rate_x = rates[i, 2 * s : 2 * s + 1, :]
    rate_y = rates[i, 2 * s + 1 : 2 * s + 2, :]
    remain = spread(1.0 - rate_x - rate_y)
    lane = lax.broadcasted_iota(jnp.int32, (1, LON), 1)
    west = flags[0, s, 0:1, pl.ds(at_lane, LON)] == 1
    pick_x = spread(jnp.where(west, lane + (LON - 1), lane + 1) & (LON - 1))
    from_south = spread(flags[0, s, 1:2, pl.ds(at_lane, LON)]) == 1
    inside = [jnp.where(i == edge, 0.0, 1.0) for edge in (0, LAT - 1)]
    rate_x = spread(rate_x)
    rate_y = spread(rate_y) * jnp.where(from_south, inside[0], inside[1])
    south, middle, north = ((i + d) & (RING - 1) for d in (-1, 0, 1))
    for g in range(0, source.shape[1], 8):
        here = source[middle, g : g + 8, :]
        side = jnp.take_along_axis(here, pick_x, axis=1)
        y_side = jnp.where(from_south, source[south, g : g + 8, :], source[north, g : g + 8, :])
        target[middle, g : g + 8, :] = remain * here + rate_x * side + rate_y * y_side


def entering():
    tail = 2 * ADVECTION_TOTAL + 1
    return ((0, 2), (2, tail), (tail, LAT // BAND))


def advect(spans, rates, flags, cells_in, cells_out, levels, ready=None):
    slots = len(spans)
    count = levels[0].shape[1]

    def enter(i):
        for h, (at, width) in enumerate(spans):
            block = cells_in[slot_rows(slots * LON * i, h, LON, slots), :]
            levels[0][i & (RING - 1), at : at + width, :] = block.T[:width]

    def leave(i):
        for h, (at, width) in enumerate(spans):
            block = levels[-1][i & (RING - 1), at : at + width, :]
            cells_out[slot_rows(slots * LON * i, h, LON, slots), 0:width] = block.T

    for level in levels[:-1]:
        level[RING - 1] = jnp.zeros((count, LON), jnp.float32)
    tail = 2 * ADVECTION_TOTAL + 1
    bands = LAT // BAND

    def step(b, guard):
        def run(stage, j):
            def every():
                for u in range(BAND):
                    stage(j * BAND + u)

            if guard:
                pl.when((j >= 0) & (j < bands))(every)
            else:
                every()

        run(leave, b - tail)
        for s in reversed(range(ADVECTION_TOTAL)):
            run(lambda i, s=s: substep(rates, flags, s, levels[s], levels[s + 1], i), b - 2 * (s + 1))
        run(enter, b)

    def guarded(b, carry):
        step(b, True)
        return carry

    def steady(b, carry):
        step(b, False)
        return carry

    for q, (start, stop) in enumerate(entering()):
        if ready is not None:
            ready(q)
        lax.fori_loop(start, stop, guarded if start < tail else steady, 0)
    lax.fori_loop(bands, bands + tail, guarded, 0)


def pick_and_turn(pick, turn, send, total):
    some = total // GROUPS
    pick(0, 0)
    pick(1, 1)

    def body(b, carry):
        i = 4 * b
        pick(i + 2, 2)
        pick(i + 3, 3)
        turn(i, 0)
        turn(i + 1, 1)
        pick(jnp.minimum(i + 4, total - 2), 0)
        pick(jnp.minimum(i + 5, total - 1), 1)
        turn(i + 2, 2)
        turn(i + 3, 3)
        return carry

    for q in range(GROUPS):
        lax.fori_loop(q * some // 4, (q + 1) * some // 4, body, 0)
        send(q).start()
    for q in range(GROUPS):
        send(q).wait()


def lay_on_grid(index, x_hbm, o_hbm, x_v, o_v, tile_a, tile_b, sem_in, sem_out):
    spans = spans_first(x_v.shape[0])
    slots = len(spans)
    tiles = (tile_a, tile_b)
    wide = CELLS // GROUPS

    def fetch(q):
        part = pl.ds(q * wide, wide)
        return pltpu.make_async_copy(x_hbm.at[:, part], x_v.at[:, part], sem_in.at[q])

    for q in range(GROUPS):
        fetch(q).start()

    def turn(c, slot):
        at_lane = pl.multiple_of(c * LANES, LANES)
        for h, (at, width) in enumerate(spans):
            block = x_v[at : at + width, pl.ds(at_lane, LANES)]
            tiles[slot][slot_rows(0, h, LANES, slots), 0:width] = block.T

    def place(c, slot):
        scatter_rows(index, c * LANES, tiles[slot], 0, o_v, slots, LANES)

    fetch(0).wait()
    turn(0, 0)

    def body(b, carry):
        c = 2 * b
        turn(c + 1, 1)
        place(c, 0)
        turn(jnp.minimum(c + 2, CELLS // LANES - 1), 0)
        place(c + 1, 1)
        return carry

    each = wide // LANES // 2
    for q in range(GROUPS):
        if q + 1 < GROUPS:
            fetch(q + 1).wait()
        lax.fori_loop(q * each, (q + 1) * each, body, 0)
    out = pltpu.make_async_copy(o_v, o_hbm, sem_out)
    out.start()
    out.wait()


def gather_rates(shared, rates, count):
    rates[...] = jnp.zeros_like(rates)
    for d in range(shared.shape[0]):
        for t in range(shared.shape[1]):
            lat = d * count // LANES + t
            rates[lat] = rates[lat] + shared[d, t]


def send_part(index, cells, o_v, o_hbm, tiles, sem_out, count, at, width):
    spans = spans_first(count)
    slots = len(spans)
    half = count // 2
    devices = o_v.shape[0]
    some = devices // GROUPS

    def pick(e, slot):
        gather_rows(index, e * count + at, cells, tiles[slot], slots, width)

    def turn(e, slot):
        rows = [tiles[slot][slot_rows(0, h, width, slots), :] for h in range(slots)]
        if is_packed(count, width):
            o_v[e] = jnp.concatenate(rows, axis=0).T[:half]
        else:
            for h in range(slots):
                o_v[e, h * half : (h + 1) * half, 0:width] = rows[h].T[:half]

    def send(q):
        part = pl.ds(q * some, some)
        return pltpu.make_async_copy(o_v.at[part], o_hbm.at[part], sem_out.at[q])

    pick_and_turn(pick, turn, send, devices)


def first_pass(count, at, width):
    def kernel(index, cells_hbm, shared, flags, o_hbm, keep_hbm, rates, cells_in, cells_out, o_v, *rest):
        tiles, (sem_out, sem_in, sem_keep), levels = rest[:4], rest[4:7], rest[7:]
        spans = spans_first(count)

        def fetch(q):
            start, stop = (len(spans) * LON * BAND * b for b in entering()[q])
            part = pl.ds(start, stop - start)
            return pltpu.make_async_copy(cells_hbm.at[part], cells_in.at[part], sem_in.at[q])

        for q in range(len(entering())):
            fetch(q).start()
        gather_rates(shared, rates, count)
        advect(spans, rates, flags, cells_in, cells_out, levels, lambda q: fetch(q).wait())
        keep = pltpu.make_async_copy(cells_out, keep_hbm, sem_keep)
        keep.start()
        send_part(index, cells_out, o_v, o_hbm, tiles, sem_out, count, at, width)
        keep.wait()

    return kernel


def first_rest(count, at, width):
    def kernel(index, cells, o_hbm, o_v, *rest):
        send_part(index, cells, o_v, o_hbm, rest[:4], rest[4], count, at, width)

    return kernel


def second_pass(count, devices, at, width):
    packed = is_packed(count, width)
    rows = count // 2 if packed else count

    def kernel(index, place, a_hbm, rates, flags, extra, *rest):
        if at:
            rest = rest[1:]
        o_hbm, a_v, cells_in, cells_out, o_v, *rest = rest
        tiles, (sem_in, sem_out), levels = rest[:4], rest[4:6], rest[6:]
        tile_a = tiles[0]
        some = devices // GROUPS

        def fetch(q):
            part = pl.ds(q * some * rows, some * rows)
            return pltpu.make_async_copy(a_hbm.at[part], a_v.at[part], sem_in.at[q])

        for q in range(GROUPS):
            fetch(q).start()

        def arrive(d, carry):
            at_row = pl.multiple_of(d * rows, 8)
            if packed:
                tile_a[0:rows, :] = pltpu.roll(a_v[pl.ds(at_row, rows), :], LANES // 2, 1)
                scatter_rows(index, d * count, a_v, at_row, cells_in, 1, rows)
                scatter_rows(index, d * count + rows, tile_a, 0, cells_in, 1, rows)
            else:
                scatter_rows(index, d * count, a_v, at_row, cells_in, 1, rows)
            return carry

        for q in range(GROUPS):
            fetch(q).wait()
            lax.fori_loop(q * some, (q + 1) * some, arrive, 0)
        advect(((0, width),), rates, flags, cells_in, cells_out, levels)
        mine = place[0] * count + at
        for u0 in range(0, width, BATCH):
            own = [pl.ds(index[mine + u], 1) for u in range(u0, u0 + BATCH)]
            sums = [cells_out[own[u], :] + extra[u0 + u : u0 + u + 1, :] for u in range(BATCH)]
            for u in range(BATCH):
                cells_out[own[u], :] = sums[u]

        def pick(c, slot):
            gather_rows(index, c * LANES, cells_out, tiles[slot], 1, LANES)

        def turn(c, slot):
            at_lane = pl.multiple_of(c * LANES, LANES)
            o_v[:, pl.ds(at_lane, LANES)] = tiles[slot][0:LANES, :].T[:width]

        wide = CELLS // GROUPS

        def send(q):
            part = pl.ds(q * wide, wide)
            return pltpu.make_async_copy(o_v.at[:, part], o_hbm.at[pl.ds(at, width), part], sem_out.at[q])

        pick_and_turn(pick, turn, send, CELLS // LANES)

    return kernel


def shards(covariance, advective_ratio, flow_heading_flags, cell_of_state, added_uncertainty):
    count = covariance.shape[0]
    devices = lax.axis_size(AXES)
    here = lax.axis_index(AXES)
    smem = pl.BlockSpec(memory_space=pltpu.SMEM)
    vmem = pl.BlockSpec(memory_space=pltpu.VMEM)
    hbm = pl.BlockSpec(memory_space=pl.ANY)
    f32 = jnp.float32
    slots = len(spans_first(count))
    cells = (slots * CELLS, LANES)
    sems = pltpu.SemaphoreType.DMA((GROUPS,))

    def levels(rows):
        return [pltpu.VMEM((RING, rows, LON), f32)] * (ADVECTION_TOTAL + 1)

    def tiles(rows):
        return [pltpu.VMEM((rows, LANES), f32)] * 4

    def params(mib):
        return pltpu.CompilerParams(vmem_limit_bytes=mib * MIB)

    def cost(us):
        return pl.CostEstimate(flops=us * 10**6, bytes_accessed=us * 3 * 10**6, transcendentals=0)

    own = advective_ratio[0].reshape(ADVECTION_TOTAL * 2, count)
    held = -(-(count + LANES - math.gcd(count, LANES)) // LANES)
    own = lax.dynamic_update_slice(
        jnp.zeros((ADVECTION_TOTAL * 2, held * LANES), f32), own, (0, count * here % LANES)
    )
    own = jnp.transpose(own.reshape(ADVECTION_TOTAL * 2, held, LANES), (1, 0, 2))
    own = jnp.broadcast_to(own[None], (devices,) + own.shape)
    shared = lax.all_to_all(own, AXES, split_axis=0, concat_axis=0, tiled=True)

    on_grid = pl.pallas_call(
        lay_on_grid,
        out_shape=jax.ShapeDtypeStruct(cells, f32),
        in_specs=[smem, hbm],
        out_specs=hbm,
        scratch_shapes=[pltpu.VMEM(covariance.shape, f32), pltpu.VMEM(cells, f32)]
        + tiles(slots * LANES)[:2]
        + [sems, pltpu.SemaphoreType.DMA(())],
        compiler_params=params(60),
        cost_estimate=cost(10),
        name="lay_on_grid",
    )(cell_of_state, covariance)

    parts = spans_second(count)
    blocks = [
        (devices, count // 2 if is_packed(count, width) else count, LANES) for _, width in parts
    ]
    moved = []
    for (at, width), shape in zip(parts, blocks):
        staging = [pltpu.VMEM(shape, f32)] + tiles(slots * LANES) + [sems]
        if at == 0:
            sent, advected, rates = pl.pallas_call(
                first_pass(count, at, width),
                out_shape=(
                    jax.ShapeDtypeStruct(shape, f32),
                    jax.ShapeDtypeStruct(cells, f32),
                    jax.ShapeDtypeStruct((LAT + held, ADVECTION_TOTAL * 2, LON), f32),
                ),
                in_specs=[smem, hbm, vmem, vmem],
                out_specs=(hbm, hbm, vmem),
                scratch_shapes=[pltpu.VMEM(cells, f32)] * 2
                + staging
                + [sems, pltpu.SemaphoreType.DMA(())]
                + levels(count),
                compiler_params=params(60),
                cost_estimate=cost(25),
                name="first_pass",
            )(cell_of_state, on_grid, shared, flow_heading_flags)
        else:
            sent = pl.pallas_call(
                first_rest(count, at, width),
                out_shape=jax.ShapeDtypeStruct(shape, f32),
                in_specs=[smem, vmem],
                out_specs=hbm,
                scratch_shapes=staging,
                compiler_params=params(60),
                cost_estimate=cost(6),
                name="first_rest",
            )(cell_of_state, advected)
        arrived = lax.all_to_all(sent, AXES, split_axis=0, concat_axis=0, tiled=True)
        moved.append(arrived.reshape(devices * shape[1], LANES))

    result = None
    for (at, width), arrived in zip(parts, moved):
        lane = lax.broadcasted_iota(jnp.int32, (width, LANES), 1)
        row = lax.broadcasted_iota(jnp.int32, (width, LANES), 0)
        extra = jnp.where(lane == row, added_uncertainty[0, at : at + width, None], 0.0)
        args = [cell_of_state, here.reshape(1), arrived, rates, flow_heading_flags, extra]
        specs = [smem, smem, hbm, vmem, vmem, vmem]
        if at:
            args.append(result)
            specs.append(hbm)
        result = pl.pallas_call(
            second_pass(count, devices, at, width),
            out_shape=jax.ShapeDtypeStruct((count, CELLS), f32),
            in_specs=specs,
            out_specs=hbm,
            scratch_shapes=[
                pltpu.VMEM(arrived.shape, f32),
                pltpu.VMEM((CELLS, LANES), f32),
                pltpu.VMEM((CELLS, LANES), f32),
                pltpu.VMEM((width, CELLS), f32),
            ]
            + tiles(LANES)
            + [sems, sems]
            + levels(width),
            input_output_aliases={6: 0} if at else {},
            compiler_params=params(60),
            cost_estimate=cost(25),
            name="second_pass",
        )(*args)
    return result


def solution(mesh):
    in_specs = (
        P(AXES, None),
        P(None, None, None, AXES),
        P(),
        P(),
        P(None, AXES),
    )
    return jax.shard_map(shards, mesh=mesh, in_specs=in_specs, out_specs=P(AXES, None), check_vma=False)
```

```python
import math

import jax
import jax.numpy as jnp
from jax import lax
from jax.experimental import pallas as pl
from jax.experimental.pallas import tpu as pltpu
from jax.sharding import PartitionSpec as P

LAT = 48
LON = 128
ADVECTION_TOTAL = 4
CELLS = LAT * LON
LANES = 128
AXES = ("row", "col")
GROUPS = 4
BATCH = 16
BAND = 2
RING = 4 * BAND
PICKED = 2 * BAND
MIB = 2**20


def spans_first(count):
    half = count // 2
    return ((0, half), (half, half))


def spans_second(count):
    return tuple((at, min(LANES, count - at)) for at in range(0, count, LANES))


def is_packed(count, width):
    return 2 * width == LANES and count > width


def block_rows(count):
    return sum(count // 2 if is_packed(count, width) else count for _, width in spans_second(count))


def slot_rows(start, h, total, slots):
    return pl.ds(start + h, total, stride=slots) if slots > 1 else pl.ds(start, total)


def gather_rows(index, start, source, target, slots, total):
    for u0 in range(0, total, BATCH):
        some = range(u0, min(u0 + BATCH, total))
        rows = [source[pl.ds(pl.multiple_of(slots * index[start + u], slots), slots), :] for u in some]
        for u, row in zip(some, rows):
            target[slots * u : slots * (u + 1), :] = row


def substep(rates, flags, s, source, target, i):
    def spread(row):
        return jnp.broadcast_to(row, (8, LON))

    at_lane = pl.multiple_of(i * LON, LON)
    rate_x = rates[i, 2 * s : 2 * s + 1, :]
    rate_y = rates[i, 2 * s + 1 : 2 * s + 2, :]
    remain = spread(1.0 - rate_x - rate_y)
    lane = lax.broadcasted_iota(jnp.int32, (1, LON), 1)
    west = flags[0, s, 0:1, pl.ds(at_lane, LON)] == 1
    pick_x = spread(jnp.where(west, lane + (LON - 1), lane + 1) & (LON - 1))
    from_south = spread(flags[0, s, 1:2, pl.ds(at_lane, LON)]) == 1
    inside = [jnp.where(i == edge, 0.0, 1.0) for edge in (0, LAT - 1)]
    rate_x = spread(rate_x)
    rate_y = spread(rate_y) * jnp.where(from_south, inside[0], inside[1])
    south, middle, north = ((i + d) & (RING - 1) for d in (-1, 0, 1))
    for g in range(0, source.shape[1], 8):
        here = source[middle, g : g + 8, :]
        side = jnp.take_along_axis(here, pick_x, axis=1)
        y_side = jnp.where(from_south, source[south, g : g + 8, :], source[north, g : g + 8, :])
        target[middle, g : g + 8, :] = remain * here + rate_x * side + rate_y * y_side


def advect(spans, state_of_cell, rates, flags, states_in, cells_out, picked, levels):
    slots = len(spans)
    count = levels[0].shape[1]
    bands = LAT // BAND
    tail = 2 * ADVECTION_TOTAL + 1

    def pick(i):
        gather_rows(state_of_cell, i * LON, states_in, picked.at[i & (PICKED - 1)], slots, LON)

    def enter(i):
        for h, (at, width) in enumerate(spans):
            block = picked.at[i & (PICKED - 1)][slot_rows(0, h, LON, slots), :]
            levels[0][i & (RING - 1), at : at + width, :] = block.T[:width]

    def leave(i):
        for h, (at, width) in enumerate(spans):
            block = levels[-1][i & (RING - 1), at : at + width, :]
            cells_out[slot_rows(slots * LON * i, h, LON, slots), 0:width] = block.T

    def step(b, guard):
        def run(stage, j):
            def every():
                for u in range(BAND):
                    stage(j * BAND + u)

            if guard:
                pl.when((j >= 0) & (j < bands))(every)
            else:
                every()

        run(leave, b - tail)
        for s in reversed(range(ADVECTION_TOTAL)):
            run(lambda i, s=s: substep(rates, flags, s, levels[s], levels[s + 1], i), b - 2 * (s + 1))
        run(enter, b)
        run(pick, b + 1 if guard else jnp.minimum(b + 1, bands - 1))

    def guarded(b, carry):
        step(b, True)
        return carry

    def steady(b, carry):
        step(b, False)
        return carry

    for level in levels[:-1]:
        level[RING - 1] = jnp.zeros((count, LON), jnp.float32)
    lax.fori_loop(-1, tail, guarded, 0)
    lax.fori_loop(tail, bands, steady, 0)
    lax.fori_loop(bands, bands + tail, guarded, 0)


def pick_and_turn(pick, turn, send, total):
    some = total // GROUPS
    pick(0, 0)
    pick(1, 1)

    def body(b, carry):
        i = 4 * b
        pick(i + 2, 2)
        pick(i + 3, 3)
        turn(i, 0)
        turn(i + 1, 1)
        pick(jnp.minimum(i + 4, total - 2), 0)
        pick(jnp.minimum(i + 5, total - 1), 1)
        turn(i + 2, 2)
        turn(i + 3, 3)
        return carry

    for q in range(GROUPS):
        lax.fori_loop(q * some // 4, (q + 1) * some // 4, body, 0)
        send(q).start()
    for q in range(GROUPS):
        send(q).wait()


def turn_rows(cell_of_state, x_hbm, o_hbm, state_of_cell, x_v, o_v, sem_in, sem_out):
    spans = spans_first(x_v.shape[0])
    slots = len(spans)
    wide = CELLS // GROUPS

    def fetch(q):
        part = pl.ds(q * wide, wide)
        return pltpu.make_async_copy(x_hbm.at[:, part], x_v.at[:, part], sem_in.at[q])

    def send(q):
        part = pl.ds(q * slots * wide, slots * wide)
        return pltpu.make_async_copy(o_v.at[part], o_hbm.at[part], sem_out.at[q])

    for q in range(GROUPS):
        fetch(q).start()

    def body(b, carry):
        for c in (2 * b, 2 * b + 1):
            at_lane = pl.multiple_of(c * LANES, LANES)
            for h, (at, width) in enumerate(spans):
                block = x_v[at : at + width, pl.ds(at_lane, LANES)]
                o_v[slot_rows(slots * LANES * c, h, LANES, slots), 0:width] = block.T
            for u in range(LANES):
                state_of_cell[cell_of_state[at_lane + u]] = at_lane + u
        return carry

    each = wide // LANES // 2
    for q in range(GROUPS):
        fetch(q).wait()
        lax.fori_loop(q * each, (q + 1) * each, body, 0)
        send(q).start()
    for q in range(GROUPS):
        send(q).wait()


def gather_rates(shared, rates, count):
    rates[...] = jnp.zeros_like(rates)
    for d in range(shared.shape[0]):
        for t in range(shared.shape[1]):
            lat = d * count // LANES + t
            rates[lat] = rates[lat] + shared[d, t]


def first_pass(
    cell_of_state, state_of_cell, states_hbm, shared, flags, o_hbm, rates, states, cells, o_v, picked, *rest
):
    tiles, (sem_in, sem_out), levels = rest[:4], rest[4:6], rest[6:]
    count = levels[0].shape[1]
    devices = o_v.shape[0]
    spans = spans_first(count)
    slots = len(spans)
    half = count // 2
    rows = slots * CELLS // GROUPS

    def fetch(q):
        part = pl.ds(q * rows, rows)
        return pltpu.make_async_copy(states_hbm.at[part], states.at[part], sem_in.at[q])

    for q in range(GROUPS):
        fetch(q).start()
    gather_rates(shared, rates, count)
    for q in range(GROUPS):
        fetch(q).wait()
    advect(spans, state_of_cell, rates, flags, states, cells, picked, levels)

    def pick(e, slot):
        gather_rows(cell_of_state, e * count, cells, tiles[slot], slots, count)

    def turn(e, slot):
        base = 0
        for at, width in spans_second(count):
            parts = [tiles[slot][slot_rows(slots * at, h, width, slots), :] for h in range(slots)]
            if is_packed(count, width):
                o_v[e, base : base + half, :] = jnp.concatenate(parts, axis=0).T[:half]
                base += half
            else:
                for h in range(slots):
                    o_v[e, base : base + half, 0:width] = parts[h].T[:half]
                    base += half

    some = devices // GROUPS

    def send(q):
        part = pl.ds(q * some, some)
        return pltpu.make_async_copy(o_v.at[part], o_hbm.at[part], sem_out.at[q])

    pick_and_turn(pick, turn, send, devices)


def second_pass(
    cell_of_state, state_of_cell, place, a_hbm, rates, flags, extra, o_hbm, states, cells, o_v, picked, *rest
):
    tiles, (sem_in, sem_out, arrived), levels = rest[:4], rest[4:7], rest[7:]
    count = levels[0].shape[1]
    spans = spans_second(count)
    slots = len(spans)
    half = count // 2

    def unpack(d, carry):
        base = 0
        for h, (_, width) in enumerate(spans):
            start = slots * count * d
            if is_packed(count, width):
                both = arrived[d, base : base + half, :]
                states[slot_rows(start, h, half, slots), :] = both
                states[slot_rows(start + slots * half, h, half, slots), :] = pltpu.roll(both, LANES // 2, 1)
                base += half
            else:
                states[slot_rows(start, h, count, slots), :] = arrived[d, base : base + count, :]
                base += count
        return carry

    some = arrived.shape[0] // GROUPS

    def fetch(q):
        part = pl.ds(q * some, some)
        return pltpu.make_async_copy(a_hbm.at[part], arrived.at[part], sem_in.at[q])

    for q in range(GROUPS):
        fetch(q).start()
    for q in range(GROUPS):
        fetch(q).wait()
        lax.fori_loop(q * some, (q + 1) * some, unpack, 0)
    advect(spans, state_of_cell, rates, flags, states, cells, picked, levels)
    mine = place[0] * count
    for u0 in range(0, count, BATCH):
        own = [pl.ds(slots * cell_of_state[mine + u] + u // LANES, 1) for u in range(u0, u0 + BATCH)]
        sums = [cells[own[u], :] + extra[u0 + u : u0 + u + 1, :] for u in range(BATCH)]
        for u in range(BATCH):
            cells[own[u], :] = sums[u]

    def pick(c, slot):
        gather_rows(cell_of_state, c * LANES, cells, tiles[slot], slots, LANES)

    def turn(c, slot):
        at_lane = pl.multiple_of(c * LANES, LANES)
        for h, (at, width) in enumerate(spans):
            o_v[at : at + width, pl.ds(at_lane, LANES)] = tiles[slot][slot_rows(0, h, LANES, slots), :].T[:width]

    wide = CELLS // GROUPS

    def send(q):
        part = pl.ds(q * wide, wide)
        return pltpu.make_async_copy(o_v.at[:, part], o_hbm.at[:, part], sem_out.at[q])

    pick_and_turn(pick, turn, send, CELLS // LANES)


def shards(covariance, advective_ratio, flow_heading_flags, cell_of_state, added_uncertainty):
    count = covariance.shape[0]
    devices = lax.axis_size(AXES)
    here = lax.axis_index(AXES)
    smem = pl.BlockSpec(memory_space=pltpu.SMEM)
    vmem = pl.BlockSpec(memory_space=pltpu.VMEM)
    hbm = pl.BlockSpec(memory_space=pl.ANY)
    f32 = jnp.float32
    first, second = len(spans_first(count)), len(spans_second(count))
    sems = pltpu.SemaphoreType.DMA((GROUPS,))

    def pass_scratch(slots, picks, out):
        rows = pltpu.VMEM((slots * CELLS, LANES), f32)
        return (
            [rows, rows, pltpu.VMEM(out, f32), pltpu.VMEM((PICKED, slots * LON, LANES), f32)]
            + [pltpu.VMEM((slots * picks, LANES), f32)] * 4
        )

    def params(mib):
        return pltpu.CompilerParams(vmem_limit_bytes=mib * MIB)

    def cost(us):
        return pl.CostEstimate(flops=us * 10**6, bytes_accessed=us * 3 * 10**6, transcendentals=0)

    levels = [pltpu.VMEM((RING, count, LON), f32)] * (ADVECTION_TOTAL + 1)

    own = advective_ratio[0].reshape(ADVECTION_TOTAL * 2, count)
    held = -(-(count + LANES - math.gcd(count, LANES)) // LANES)
    own = lax.dynamic_update_slice(
        jnp.zeros((ADVECTION_TOTAL * 2, held * LANES), f32), own, (0, count * here % LANES)
    )
    own = jnp.transpose(own.reshape(ADVECTION_TOTAL * 2, held, LANES), (1, 0, 2))
    own = jnp.broadcast_to(own[None], (devices,) + own.shape)
    shared = lax.all_to_all(own, AXES, split_axis=0, concat_axis=0, tiled=True)

    states = jax.ShapeDtypeStruct((first * CELLS, LANES), f32)
    turned, state_of_cell = pl.pallas_call(
        turn_rows,
        out_shape=(states, jax.ShapeDtypeStruct((CELLS,), jnp.int32)),
        in_specs=[smem, hbm],
        out_specs=(hbm, smem),
        scratch_shapes=[pltpu.VMEM(covariance.shape, f32), pltpu.VMEM(states.shape, f32), sems, sems],
        compiler_params=params(60),
        cost_estimate=cost(10),
        name="turn_rows",
    )(cell_of_state, covariance)

    shape = (devices, block_rows(count), LANES)
    sent, rates = pl.pallas_call(
        first_pass,
        out_shape=(
            jax.ShapeDtypeStruct(shape, f32),
            jax.ShapeDtypeStruct((LAT + held, ADVECTION_TOTAL * 2, LON), f32),
        ),
        in_specs=[smem, smem, hbm, vmem, vmem],
        out_specs=(hbm, vmem),
        scratch_shapes=pass_scratch(first, count, shape) + [sems, sems] + levels,
        compiler_params=params(60),
        cost_estimate=cost(25),
        name="first_pass",
    )(cell_of_state, state_of_cell, turned, shared, flow_heading_flags)
    arrived = lax.all_to_all(sent, AXES, split_axis=0, concat_axis=0, tiled=True)

    lane = lax.broadcasted_iota(jnp.int32, (count, LANES), 1)
    row = lax.broadcasted_iota(jnp.int32, (count, LANES), 0)
    extra = jnp.where(lane == row % LANES, added_uncertainty[0][:, None], 0.0)
    return pl.pallas_call(
        second_pass,
        out_shape=jax.ShapeDtypeStruct((count, CELLS), f32),
        in_specs=[smem, smem, smem, hbm, vmem, vmem, vmem],
        out_specs=hbm,
        scratch_shapes=pass_scratch(second, LANES, (count, CELLS))
        + [sems, sems, pltpu.VMEM(shape, f32)]
        + levels,
        compiler_params=params(60),
        cost_estimate=cost(25),
        name="second_pass",
    )(cell_of_state, state_of_cell, here.reshape(1), arrived, rates, flow_heading_flags, extra)


def solution(mesh):
    in_specs = (
        P(AXES, None),
        P(None, None, None, AXES),
        P(),
        P(),
        P(None, AXES),
    )
    return jax.shard_map(shards, mesh=mesh, in_specs=in_specs, out_specs=P(AXES, None), check_vma=False)
```

```python
import math

import jax
import jax.numpy as jnp
from jax import lax
from jax.experimental import pallas as pl
from jax.experimental.pallas import tpu as pltpu
from jax.sharding import PartitionSpec as P

LAT = 48
LON = 128
ADVECTION_TOTAL = 4
CELLS = LAT * LON
LANES = 128
AXES = ("row", "col")
GROUPS = 4
BATCH = 16
BAND = 8
TURNS = 4
MIB = 2**20


def spans_first(count):
    half = count // 2
    return ((0, half), (half, half))


def spans_second(count):
    return tuple((at, min(LANES, count - at)) for at in range(0, count, LANES))


def is_packed(count, width):
    return 2 * width == LANES and count > width


def block_rows(count):
    return sum(count // 2 if is_packed(count, width) else count for _, width in spans_second(count))


def slot_rows(start, h, total, slots):
    return pl.ds(start + h, total, stride=slots) if slots > 1 else pl.ds(start, total)


def scatter_rows(index, start, source, target, slots, total):
    for u0 in range(0, total, BATCH):
        some = range(u0, min(u0 + BATCH, total))
        rows = [source[slots * u : slots * (u + 1), :] for u in some]
        for u, row in zip(some, rows):
            target[pl.ds(pl.multiple_of(slots * index[start + u], slots), slots), :] = row


def fill_and_place(fill, place, start, stop, last):
    def body(b, carry):
        i = 2 * b
        fill(i + 1, 1)
        place(i, 0)
        fill(jnp.minimum(i + 2, last), 0)
        place(i + 1, 1)
        return carry

    lax.fori_loop(start // 2, stop // 2, body, 0)


def substep(rates, flags, s, source, target, i):
    def spread(row):
        return jnp.broadcast_to(row, (8, LON))

    at_lane = pl.multiple_of(i * LON, LON)
    rate_x = rates[i, 2 * s : 2 * s + 1, :]
    rate_y = rates[i, 2 * s + 1 : 2 * s + 2, :]
    remain = spread(1.0 - rate_x - rate_y)
    lane = lax.broadcasted_iota(jnp.int32, (1, LON), 1)
    west = flags[0, s, 0:1, pl.ds(at_lane, LON)] == 1
    pick_x = spread(jnp.where(west, lane + (LON - 1), lane + 1) & (LON - 1))
    from_south = spread(flags[0, s, 1:2, pl.ds(at_lane, LON)]) == 1
    rate_x, rate_y = spread(rate_x), spread(rate_y)
    for g in range(0, source.shape[1], 8):
        here = source[i + 1, g : g + 8, :]
        side = jnp.take_along_axis(here, pick_x, axis=1)
        y_side = jnp.where(from_south, source[i, g : g + 8, :], source[i + 2, g : g + 8, :])
        target[i + 1, g : g + 8, :] = remain * here + rate_x * side + rate_y * y_side


def advect(spans, state_of_cell, rates, flags, packed, tiles, level_a, level_b):
    slots = len(spans)
    count = level_a.shape[1]

    def enter(b, carry):
        for i in range(TURNS):
            for h, (at, width) in enumerate(spans):
                block = packed[slot_rows(slots * LON * (TURNS * b + i), h, LON, slots), :]
                level_a[TURNS * b + i + 1, at : at + width, :] = block.T[:width]
        return carry

    lax.fori_loop(0, LAT // TURNS, enter, 0)
    for level in (level_a, level_b):
        for edge in (0, LAT + 1):
            level[edge] = jnp.zeros((count, LON), jnp.float32)
    source, target = level_a, level_b
    for s in range(ADVECTION_TOTAL):

        def band(b, carry, s=s, source=source, target=target):
            for i in range(BAND):
                substep(rates, flags, s, source, target, b * BAND + i)
            return carry

        lax.fori_loop(0, LAT // BAND, band, 0)
        source, target = target, source

    def leave(i, slot, final=source):
        for h, (at, width) in enumerate(spans):
            tiles[slot][slot_rows(0, h, LON, slots), 0:width] = final[i + 1, at : at + width, :].T

    def place(i, slot):
        scatter_rows(state_of_cell, i * LON, tiles[slot], packed, slots, LON)

    leave(0, 0)
    fill_and_place(leave, place, 0, LAT, LAT - 1)


def invert(cell_of_state, state_of_cell):
    unroll = 64

    def body(b, carry):
        for u in range(unroll):
            state_of_cell[cell_of_state[b * unroll + u]] = b * unroll + u
        return carry

    lax.fori_loop(0, CELLS // unroll, body, 0)


def gather_rates(shared, rates, count):
    rates[...] = jnp.zeros_like(rates)
    for d in range(shared.shape[0]):
        for t in range(shared.shape[1]):
            lat = d * count // LANES + t
            rates[lat] = rates[lat] + shared[d, t]


def first_pass(
    cell_of_state, state_of_cell, x_hbm, shared, flags, o_hbm, rates, x_v, packed, o_v, tile_a, tile_b, *rest
):
    (sem_in, sem_out), levels = rest[:2], rest[2:]
    tiles = (tile_a, tile_b)
    count = x_v.shape[0]
    devices = o_v.shape[0]
    spans = spans_first(count)
    slots = len(spans)
    half = count // 2
    wide = CELLS // GROUPS

    def fetch(q):
        part = pl.ds(q * wide, wide)
        return pltpu.make_async_copy(x_hbm.at[:, part], x_v.at[:, part], sem_in.at[q])

    for q in range(GROUPS):
        fetch(q).start()
    gather_rates(shared, rates, count)

    def turn(c, slot):
        at_lane = pl.multiple_of(c * LANES, LANES)
        for h, (at, width) in enumerate(spans):
            block = x_v[at : at + width, pl.ds(at_lane, LANES)]
            tiles[slot][slot_rows(0, h, LANES, slots), 0:width] = block.T

    def place(c, slot):
        scatter_rows(cell_of_state, c * LANES, tiles[slot], packed, slots, LANES)

    each = wide // LANES
    fetch(0).wait()
    turn(0, 0)
    for q in range(GROUPS):
        if q + 1 < GROUPS:
            fetch(q + 1).wait()
        fill_and_place(turn, place, q * each, (q + 1) * each, CELLS // LANES - 1)
    advect(spans, state_of_cell, rates, flags, packed, tiles, *levels)

    def pack(e):
        base = 0
        for at, width in spans_second(count):
            start = slots * (e * count + at)
            parts = [packed[slot_rows(start, h, width, slots), :] for h in range(slots)]
            if is_packed(count, width):
                o_v[e, base : base + half, :] = jnp.concatenate(parts, axis=0).T[:half]
                base += half
            else:
                for h in range(slots):
                    o_v[e, base : base + half, 0:width] = parts[h].T[:half]
                    base += half

    def pack_two(b, carry):
        pack(2 * b)
        pack(2 * b + 1)
        return carry

    some = devices // GROUPS

    def send(q):
        part = pl.ds(q * some, some)
        return pltpu.make_async_copy(o_v.at[part], o_hbm.at[part], sem_out.at[q])

    for q in range(GROUPS):
        lax.fori_loop(q * some // 2, (q + 1) * some // 2, pack_two, 0)
        send(q).start()
    for q in range(GROUPS):
        send(q).wait()


def second_pass(
    cell_of_state, state_of_cell, place, a_hbm, rates, flags, extra, o_hbm, a_v, packed, o_v, tile_a, tile_b, *rest
):
    (sem_in, sem_out), levels = rest[:2], rest[2:]
    tiles = (tile_a, tile_b)
    count = o_v.shape[0]
    devices = a_v.shape[0]
    spans = spans_second(count)
    slots = len(spans)
    half = count // 2
    some = devices // GROUPS

    def fetch(q):
        part = pl.ds(q * some, some)
        return pltpu.make_async_copy(a_hbm.at[part], a_v.at[part], sem_in.at[q])

    for q in range(GROUPS):
        fetch(q).start()

    def unpack(d, slot):
        tile = tiles[slot]
        base = 0
        for h, (_, width) in enumerate(spans):
            if is_packed(count, width):
                both = a_v[d, base : base + half, :]
                tile[slot_rows(0, h, half, slots), :] = both
                tile[slot_rows(slots * half, h, half, slots), :] = pltpu.roll(both, LANES // 2, 1)
                base += half
            else:
                tile[slot_rows(0, h, count, slots), :] = a_v[d, base : base + count, :]
                base += count

    def lay(d, slot):
        scatter_rows(cell_of_state, d * count, tiles[slot], packed, slots, count)

    fetch(0).wait()
    unpack(0, 0)
    for q in range(GROUPS):
        if q + 1 < GROUPS:
            fetch(q + 1).wait()
        fill_and_place(unpack, lay, q * some, (q + 1) * some, devices - 1)
    advect(spans, state_of_cell, rates, flags, packed, tiles, *levels)
    mine = pl.ds(pl.multiple_of(slots * count * place[0], 8), slots * count)
    packed[mine, :] = packed[mine, :] + extra[...]

    def turn(b, carry):
        for i in range(TURNS):
            c = TURNS * b + i
            at_lane = pl.multiple_of(c * LANES, LANES)
            for h, (at, width) in enumerate(spans):
                block = packed[slot_rows(slots * LANES * c, h, LANES, slots), :]
                o_v[at : at + width, pl.ds(at_lane, LANES)] = block.T[:width]
        return carry

    wide = CELLS // GROUPS

    def send(q):
        part = pl.ds(q * wide, wide)
        return pltpu.make_async_copy(o_v.at[:, part], o_hbm.at[:, part], sem_out.at[q])

    each = wide // LANES // TURNS
    for q in range(GROUPS):
        lax.fori_loop(q * each, (q + 1) * each, turn, 0)
        send(q).start()
    for q in range(GROUPS):
        send(q).wait()


def shards(covariance, advective_ratio, flow_heading_flags, cell_of_state, added_uncertainty):
    count = covariance.shape[0]
    devices = lax.axis_size(AXES)
    here = lax.axis_index(AXES)
    smem = pl.BlockSpec(memory_space=pltpu.SMEM)
    vmem = pl.BlockSpec(memory_space=pltpu.VMEM)
    hbm = pl.BlockSpec(memory_space=pl.ANY)
    f32 = jnp.float32
    first, second = len(spans_first(count)), len(spans_second(count))
    sems = pltpu.SemaphoreType.DMA((GROUPS,))

    def pass_scratch(slots, first_shape, last_shape):
        tile = pltpu.VMEM((slots * max(count, LANES), LANES), f32)
        level = pltpu.VMEM((LAT + 2, count, LON), f32)
        packed = pltpu.VMEM((slots * CELLS, LANES), f32)
        return [
            pltpu.VMEM(first_shape, f32),
            packed,
            pltpu.VMEM(last_shape, f32),
            tile,
            tile,
            sems,
            sems,
            level,
            level,
        ]

    def params(mib):
        return pltpu.CompilerParams(vmem_limit_bytes=mib * MIB)

    def cost(us):
        return pl.CostEstimate(flops=us * 10**6, bytes_accessed=us * 3 * 10**6, transcendentals=0)

    own = advective_ratio[0].reshape(ADVECTION_TOTAL * 2, count)
    held = -(-(count + LANES - math.gcd(count, LANES)) // LANES)
    own = lax.dynamic_update_slice(
        jnp.zeros((ADVECTION_TOTAL * 2, held * LANES), f32), own, (0, count * here % LANES)
    )
    own = jnp.transpose(own.reshape(ADVECTION_TOTAL * 2, held, LANES), (1, 0, 2))
    own = jnp.broadcast_to(own[None], (devices,) + own.shape)
    shared = lax.all_to_all(own, AXES, split_axis=0, concat_axis=0, tiled=True)

    state_of_cell = pl.pallas_call(
        invert,
        out_shape=jax.ShapeDtypeStruct((CELLS,), jnp.int32),
        in_specs=[smem],
        out_specs=smem,
        cost_estimate=cost(10),
        name="invert",
    )(cell_of_state)

    shape = (devices, block_rows(count), LANES)
    sent, rates = pl.pallas_call(
        first_pass,
        out_shape=(
            jax.ShapeDtypeStruct(shape, f32),
            jax.ShapeDtypeStruct((LAT + held, ADVECTION_TOTAL * 2, LON), f32),
        ),
        in_specs=[smem, smem, hbm, vmem, vmem],
        out_specs=(hbm, vmem),
        scratch_shapes=pass_scratch(first, covariance.shape, shape),
        compiler_params=params(60),
        cost_estimate=cost(25),
        name="first_pass",
    )(cell_of_state, state_of_cell, covariance, shared, flow_heading_flags)
    arrived = lax.all_to_all(sent, AXES, split_axis=0, concat_axis=0, tiled=True)

    row = lax.broadcasted_iota(jnp.int32, (count, second, LANES), 0)
    slot = lax.broadcasted_iota(jnp.int32, (count, second, LANES), 1) * LANES
    slot = slot + lax.broadcasted_iota(jnp.int32, (count, second, LANES), 2)
    extra = jnp.where(row == slot, added_uncertainty[0][:, None, None], 0.0).reshape(second * count, LANES)
    return pl.pallas_call(
        second_pass,
        out_shape=jax.ShapeDtypeStruct((count, CELLS), f32),
        in_specs=[smem, smem, smem, hbm, vmem, vmem, vmem],
        out_specs=hbm,
        scratch_shapes=pass_scratch(second, shape, (count, CELLS)),
        compiler_params=params(60),
        cost_estimate=cost(25),
        name="second_pass",
    )(cell_of_state, state_of_cell, here.reshape(1), arrived, rates, flow_heading_flags, extra)


def solution(mesh):
    in_specs = (
        P(AXES, None),
        P(None, None, None, AXES),
        P(),
        P(),
        P(None, AXES),
    )
    return jax.shard_map(shards, mesh=mesh, in_specs=in_specs, out_specs=P(AXES, None), check_vma=False)
```

```python
import math

import jax
import jax.numpy as jnp
from jax import lax
from jax.experimental import pallas as pl
from jax.experimental.pallas import tpu as pltpu
from jax.sharding import PartitionSpec as P

LAT = 48
LON = 128
ADVECTION_TOTAL = 4
CELLS = LAT * LON
LANES = 128
AXES = ("row", "col")
GROUPS = 8
BATCH = 16
BAND = 16
TURNS = 6
MIB = 2**20


def spans_first(count):
    half = count // 2
    return ((0, half), (half, half))


def spans_second(count):
    return tuple((at, min(LANES, count - at)) for at in range(0, count, LANES))


def is_packed(count, width):
    return 2 * width == LANES and count > width


def block_rows(count):
    return sum(count // 2 if is_packed(count, width) else count for _, width in spans_second(count))


def slot_rows(start, h, total, slots):
    return pl.ds(start + h, total, stride=slots) if slots > 1 else pl.ds(start, total)


def scatter_rows(index, start, source, target, slots, total):
    for u0 in range(0, total, BATCH):
        some = range(u0, min(u0 + BATCH, total))
        rows = [source[slots * u : slots * (u + 1), :] for u in some]
        for u, row in zip(some, rows):
            target[pl.ds(pl.multiple_of(index[start + u], slots), slots), :] = row


def fill_and_place(fill, place, start, stop, last):
    def body(b, carry):
        i = 2 * b
        fill(i + 1, 1)
        place(i, 0)
        fill(jnp.minimum(i + 2, last), 0)
        place(i + 1, 1)
        return carry

    lax.fori_loop(start // 2, stop // 2, body, 0)


def substep(rates, flags, s, source, target, i):
    def spread(row):
        return jnp.broadcast_to(row, (8, LON))

    at_lane = pl.multiple_of(i * LON, LON)
    rate_x = rates[i, 2 * s : 2 * s + 1, :]
    rate_y = rates[i, 2 * s + 1 : 2 * s + 2, :]
    remain = spread(1.0 - rate_x - rate_y)
    lane = lax.broadcasted_iota(jnp.int32, (1, LON), 1)
    west = flags[0, s, 0:1, pl.ds(at_lane, LON)] == 1
    pick_x = spread(jnp.where(west, lane + (LON - 1), lane + 1) & (LON - 1))
    from_south = spread(flags[0, s, 1:2, pl.ds(at_lane, LON)]) == 1
    rate_x, rate_y = spread(rate_x), spread(rate_y)
    for g in range(0, source.shape[1], 8):
        here = source[i + 1, g : g + 8, :]
        side = jnp.take_along_axis(here, pick_x, axis=1)
        y_side = jnp.where(from_south, source[i, g : g + 8, :], source[i + 2, g : g + 8, :])
        target[i + 1, g : g + 8, :] = remain * here + rate_x * side + rate_y * y_side


def advect(spans, state_of_cell, rates, flags, packed, tiles, level_a, level_b):
    slots = len(spans)
    count = level_a.shape[1]

    def enter(b, carry):
        for i in range(TURNS):
            for h, (at, width) in enumerate(spans):
                block = packed[slot_rows(slots * LON * (TURNS * b + i), h, LON, slots), :]
                level_a[TURNS * b + i + 1, at : at + width, :] = block.T[:width]
        return carry

    lax.fori_loop(0, LAT // TURNS, enter, 0)
    for level in (level_a, level_b):
        for edge in (0, LAT + 1):
            level[edge] = jnp.zeros((count, LON), jnp.float32)
    source, target = level_a, level_b
    for s in range(ADVECTION_TOTAL):

        def band(b, carry, s=s, source=source, target=target):
            for i in range(BAND):
                substep(rates, flags, s, source, target, b * BAND + i)
            return carry

        lax.fori_loop(0, LAT // BAND, band, 0)
        source, target = target, source

    def leave(i, slot, final=source):
        for h, (at, width) in enumerate(spans):
            tiles[slot][slot_rows(0, h, LON, slots), 0:width] = final[i + 1, at : at + width, :].T

    def place(i, slot):
        scatter_rows(state_of_cell, i * LON, tiles[slot], packed, slots, LON)

    leave(0, 0)
    fill_and_place(leave, place, 0, LAT, LAT - 1)


def invert(slots):
    unroll = 64

    def kernel(cell_of_state, state_of_cell):
        def body(b, carry):
            for u in range(unroll):
                state_of_cell[cell_of_state[b * unroll + u]] = slots * (b * unroll + u)
            return carry

        lax.fori_loop(0, CELLS // unroll, body, 0)

    return kernel


def gather_rates(shared, rates, count):
    rates[...] = jnp.zeros_like(rates)
    for d in range(shared.shape[0]):
        for t in range(shared.shape[1]):
            lat = d * count // LANES + t
            rates[lat] = rates[lat] + shared[d, t]


def first_pass(
    cell_of_state, state_of_cell, x_hbm, shared, flags, o_hbm, rates, x_v, packed, o_v, tile_a, tile_b, *rest
):
    (sem_in, sem_out), levels = rest[:2], rest[2:]
    tiles = (tile_a, tile_b)
    count = x_v.shape[0]
    devices = o_v.shape[0]
    spans = spans_first(count)
    slots = len(spans)
    half = count // 2
    wide = CELLS // GROUPS

    def fetch(q):
        part = pl.ds(q * wide, wide)
        return pltpu.make_async_copy(x_hbm.at[:, part], x_v.at[:, part], sem_in.at[q])

    for q in range(GROUPS):
        fetch(q).start()
    gather_rates(shared, rates, count)

    def turn(c, slot):
        at_lane = pl.multiple_of(c * LANES, LANES)
        for h, (at, width) in enumerate(spans):
            block = x_v[at : at + width, pl.ds(at_lane, LANES)]
            tiles[slot][slot_rows(0, h, LANES, slots), 0:width] = block.T

    def place(c, slot):
        scatter_rows(cell_of_state, c * LANES, tiles[slot], packed, slots, LANES)

    each = wide // LANES
    fetch(0).wait()
    turn(0, 0)
    for q in range(GROUPS):
        if q + 1 < GROUPS:
            fetch(q + 1).wait()
        fill_and_place(turn, place, q * each, (q + 1) * each, CELLS // LANES - 1)
    advect(spans, state_of_cell, rates, flags, packed, tiles, *levels)

    def pack(e):
        base = 0
        for at, width in spans_second(count):
            start = slots * (e * count + at)
            parts = [packed[slot_rows(start, h, width, slots), :] for h in range(slots)]
            if is_packed(count, width):
                o_v[e, base : base + half, :] = jnp.concatenate(parts, axis=0).T[:half]
                base += half
            else:
                for h in range(slots):
                    o_v[e, base : base + half, 0:width] = parts[h].T[:half]
                    base += half

    def pack_two(b, carry):
        pack(2 * b)
        pack(2 * b + 1)
        return carry

    some = devices // GROUPS

    def send(q):
        part = pl.ds(q * some, some)
        return pltpu.make_async_copy(o_v.at[part], o_hbm.at[part], sem_out.at[q])

    for q in range(GROUPS):
        lax.fori_loop(q * some // 2, (q + 1) * some // 2, pack_two, 0)
        send(q).start()
    for q in range(GROUPS):
        send(q).wait()


def second_pass(
    cell_of_state, state_of_cell, place, a_hbm, rates, flags, extra, o_hbm, a_v, packed, o_v, tile_a, tile_b, *rest
):
    (sem_in, sem_out), levels = rest[:2], rest[2:]
    tiles = (tile_a, tile_b)
    count = o_v.shape[0]
    devices = a_v.shape[0]
    spans = spans_second(count)
    slots = len(spans)
    half = count // 2
    some = devices // GROUPS

    def fetch(q):
        part = pl.ds(q * some, some)
        return pltpu.make_async_copy(a_hbm.at[part], a_v.at[part], sem_in.at[q])

    for q in range(GROUPS):
        fetch(q).start()

    def unpack(d, slot):
        tile = tiles[slot]
        base = 0
        for h, (_, width) in enumerate(spans):
            if is_packed(count, width):
                both = a_v[d, base : base + half, :]
                tile[slot_rows(0, h, half, slots), :] = both
                tile[slot_rows(slots * half, h, half, slots), :] = pltpu.roll(both, LANES // 2, 1)
                base += half
            else:
                tile[slot_rows(0, h, count, slots), :] = a_v[d, base : base + count, :]
                base += count

    def lay(d, slot):
        scatter_rows(cell_of_state, d * count, tiles[slot], packed, slots, count)

    fetch(0).wait()
    unpack(0, 0)
    for q in range(GROUPS):
        if q + 1 < GROUPS:
            fetch(q + 1).wait()
        fill_and_place(unpack, lay, q * some, (q + 1) * some, devices - 1)
    advect(spans, state_of_cell, rates, flags, packed, tiles, *levels)
    mine = pl.ds(pl.multiple_of(slots * count * place[0], 8), slots * count)
    packed[mine, :] = packed[mine, :] + extra[...]

    def turn(b, carry):
        for i in range(TURNS):
            c = TURNS * b + i
            at_lane = pl.multiple_of(c * LANES, LANES)
            for h, (at, width) in enumerate(spans):
                block = packed[slot_rows(slots * LANES * c, h, LANES, slots), :]
                o_v[at : at + width, pl.ds(at_lane, LANES)] = block.T[:width]
        return carry

    wide = CELLS // GROUPS

    def send(q):
        part = pl.ds(q * wide, wide)
        return pltpu.make_async_copy(o_v.at[:, part], o_hbm.at[:, part], sem_out.at[q])

    each = wide // LANES // TURNS
    for q in range(GROUPS):
        lax.fori_loop(q * each, (q + 1) * each, turn, 0)
        send(q).start()
    for q in range(GROUPS):
        send(q).wait()


def shards(covariance, advective_ratio, flow_heading_flags, cell_of_state, added_uncertainty):
    count = covariance.shape[0]
    devices = lax.axis_size(AXES)
    here = lax.axis_index(AXES)
    smem = pl.BlockSpec(memory_space=pltpu.SMEM)
    vmem = pl.BlockSpec(memory_space=pltpu.VMEM)
    hbm = pl.BlockSpec(memory_space=pl.ANY)
    f32 = jnp.float32
    first, second = len(spans_first(count)), len(spans_second(count))
    sems = pltpu.SemaphoreType.DMA((GROUPS,))

    def pass_scratch(slots, first_shape, last_shape):
        tile = pltpu.VMEM((slots * max(count, LANES), LANES), f32)
        level = pltpu.VMEM((LAT + 2, count, LON), f32)
        packed = pltpu.VMEM((slots * CELLS, LANES), f32)
        return [
            pltpu.VMEM(first_shape, f32),
            packed,
            pltpu.VMEM(last_shape, f32),
            tile,
            tile,
            sems,
            sems,
            level,
            level,
        ]

    def params(mib):
        return pltpu.CompilerParams(vmem_limit_bytes=mib * MIB)

    def cost(us):
        return pl.CostEstimate(flops=us * 10**6, bytes_accessed=us * 3 * 10**6, transcendentals=0)

    own = advective_ratio[0].reshape(ADVECTION_TOTAL * 2, count)
    held = -(-(count + LANES - math.gcd(count, LANES)) // LANES)
    own = lax.dynamic_update_slice(
        jnp.zeros((ADVECTION_TOTAL * 2, held * LANES), f32), own, (0, count * here % LANES)
    )
    own = jnp.transpose(own.reshape(ADVECTION_TOTAL * 2, held, LANES), (1, 0, 2))
    own = jnp.broadcast_to(own[None], (devices,) + own.shape)
    shared = lax.all_to_all(own, AXES, split_axis=0, concat_axis=0, tiled=True)

    cells_first = first * cell_of_state
    states_first = pl.pallas_call(
        invert(first),
        out_shape=jax.ShapeDtypeStruct((CELLS,), jnp.int32),
        in_specs=[smem],
        out_specs=smem,
        cost_estimate=cost(10),
        name="invert",
    )(cell_of_state)

    shape = (devices, block_rows(count), LANES)
    sent, rates = pl.pallas_call(
        first_pass,
        out_shape=(
            jax.ShapeDtypeStruct(shape, f32),
            jax.ShapeDtypeStruct((LAT + held, ADVECTION_TOTAL * 2, LON), f32),
        ),
        in_specs=[smem, smem, hbm, vmem, vmem],
        out_specs=(hbm, vmem),
        scratch_shapes=pass_scratch(first, covariance.shape, shape),
        compiler_params=params(60),
        cost_estimate=cost(25),
        name="first_pass",
    )(cells_first, states_first, covariance, shared, flow_heading_flags)
    arrived = lax.all_to_all(sent, AXES, split_axis=0, concat_axis=0, tiled=True)

    row = lax.broadcasted_iota(jnp.int32, (count, second, LANES), 0)
    slot = lax.broadcasted_iota(jnp.int32, (count, second, LANES), 1) * LANES
    slot = slot + lax.broadcasted_iota(jnp.int32, (count, second, LANES), 2)
    extra = jnp.where(row == slot, added_uncertainty[0][:, None, None], 0.0).reshape(second * count, LANES)
    cells_second, states_second = cells_first, states_first
    if first != second:
        cells_second, states_second = second * cell_of_state, states_first // first * second
    return pl.pallas_call(
        second_pass,
        out_shape=jax.ShapeDtypeStruct((count, CELLS), f32),
        in_specs=[smem, smem, smem, hbm, vmem, vmem, vmem],
        out_specs=hbm,
        scratch_shapes=pass_scratch(second, shape, (count, CELLS)),
        compiler_params=params(60),
        cost_estimate=cost(25),
        name="second_pass",
    )(cells_second, states_second, here.reshape(1), arrived, rates, flow_heading_flags, extra)


def solution(mesh):
    in_specs = (
        P(AXES, None),
        P(None, None, None, AXES),
        P(),
        P(),
        P(None, AXES),
    )
    return jax.shard_map(shards, mesh=mesh, in_specs=in_specs, out_specs=P(AXES, None), check_vma=False)
```

```python
import math

import jax
import jax.numpy as jnp
from jax import lax
from jax.experimental import pallas as pl
from jax.experimental.pallas import tpu as pltpu
from jax.sharding import PartitionSpec as P

LAT = 48
LON = 128
ADVECTION_TOTAL = 4
CELLS = LAT * LON
LANES = 128
AXES = ("row", "col")
GROUPS = 8
BATCH = 16
BAND = 16
TURNS = 6
MIB = 2**20


def spans_first(count):
    half = count // 2
    return ((0, half), (half, half))


def spans_second(count):
    return tuple((at, min(LANES, count - at)) for at in range(0, count, LANES))


def is_packed(count, width):
    return 2 * width == LANES and count > width


def block_rows(count):
    return sum(count // 2 if is_packed(count, width) else count for _, width in spans_second(count))


def slot_rows(start, h, total, slots):
    return pl.ds(start + h, total, stride=slots) if slots > 1 else pl.ds(start, total)


def scatter_rows(index, start, source, target, slots, total):
    for u0 in range(0, total, BATCH):
        some = range(u0, min(u0 + BATCH, total))
        rows = [source[slots * u : slots * (u + 1), :] for u in some]
        for u, row in zip(some, rows):
            target[pl.ds(pl.multiple_of(index[start + u], slots), slots), :] = row


def fill_and_place(fill, place, start, stop, last):
    def body(b, carry):
        i = 2 * b
        fill(i + 1, 1)
        place(i, 0)
        fill(jnp.minimum(i + 2, last), 0)
        place(i + 1, 1)
        return carry

    lax.fori_loop(start // 2, stop // 2, body, 0)


def substep(rates, flags, s, source, target, i):
    def spread(row):
        return jnp.broadcast_to(row, (8, LON))

    at_lane = pl.multiple_of(i * LON, LON)
    rate_x = rates[i, 2 * s : 2 * s + 1, :]
    rate_y = rates[i, 2 * s + 1 : 2 * s + 2, :]
    remain = spread(1.0 - rate_x - rate_y)
    lane = lax.broadcasted_iota(jnp.int32, (1, LON), 1)
    west = flags[0, s, 0:1, pl.ds(at_lane, LON)] == 1
    pick_x = spread(jnp.where(west, lane + (LON - 1), lane + 1) & (LON - 1))
    from_south = spread(flags[0, s, 1:2, pl.ds(at_lane, LON)]) == 1
    rate_x, rate_y = spread(rate_x), spread(rate_y)
    for g in range(0, source.shape[1], 8):
        here = source[i + 1, g : g + 8, :]
        side = jnp.take_along_axis(here, pick_x, axis=1)
        y_side = jnp.where(from_south, source[i, g : g + 8, :], source[i + 2, g : g + 8, :])
        target[i + 1, g : g + 8, :] = remain * here + rate_x * side + rate_y * y_side


def advect(spans, state_of_cell, rates, flags, packed, tiles, level_a, level_b, aside=None):
    slots = len(spans)
    count = level_a.shape[1]

    def enter(b, carry):
        for i in range(TURNS):
            for h, (at, width) in enumerate(spans):
                block = packed[slot_rows(slots * LON * (TURNS * b + i), h, LON, slots), :]
                level_a[TURNS * b + i + 1, at : at + width, :] = block.T[:width]
        return carry

    lax.fori_loop(0, LAT // TURNS, enter, 0)
    for level in (level_a, level_b):
        for edge in (0, LAT + 1):
            level[edge] = jnp.zeros((count, LON), jnp.float32)
    source, target = level_a, level_b
    for s in range(ADVECTION_TOTAL):

        def band(b, carry, s=s, source=source, target=target):
            for i in range(BAND):
                substep(rates, flags, s, source, target, b * BAND + i)
            if aside is not None:
                aside(b + s * (LAT // BAND))
            return carry

        lax.fori_loop(0, LAT // BAND, band, 0)
        source, target = target, source

    def leave(i, slot, final=source):
        for h, (at, width) in enumerate(spans):
            tiles[slot][slot_rows(0, h, LON, slots), 0:width] = final[i + 1, at : at + width, :].T

    def place(i, slot):
        scatter_rows(state_of_cell, i * LON, tiles[slot], packed, slots, LON)

    leave(0, 0)
    fill_and_place(leave, place, 0, LAT, LAT - 1)


def gather_rates(shared, rates, count):
    rates[...] = jnp.zeros_like(rates)
    for d in range(shared.shape[0]):
        for t in range(shared.shape[1]):
            lat = d * count // LANES + t
            rates[lat] = rates[lat] + shared[d, t]


def first_pass(
    cell_of_state, cells, x_hbm, shared, flags, o_hbm, rates, state_of_cell, x_v, packed, o_v, tile_a, tile_b, *rest
):
    (sem_in, sem_out), levels = rest[:2], rest[2:]
    tiles = (tile_a, tile_b)
    count = x_v.shape[0]
    devices = o_v.shape[0]
    spans = spans_first(count)
    slots = len(spans)
    half = count // 2
    wide = CELLS // GROUPS

    def fetch(q):
        part = pl.ds(q * wide, wide)
        return pltpu.make_async_copy(x_hbm.at[:, part], x_v.at[:, part], sem_in.at[q])

    for q in range(GROUPS):
        fetch(q).start()
    gather_rates(shared, rates, count)

    def turn(c, slot):
        at_lane = pl.multiple_of(c * LANES, LANES)
        for h, (at, width) in enumerate(spans):
            block = x_v[at : at + width, pl.ds(at_lane, LANES)]
            tiles[slot][slot_rows(0, h, LANES, slots), 0:width] = block.T

    def place(c, slot):
        scatter_rows(cell_of_state, c * LANES, tiles[slot], packed, slots, LANES)

    each = wide // LANES
    fetch(0).wait()
    turn(0, 0)
    for q in range(GROUPS):
        if q + 1 < GROUPS:
            fetch(q + 1).wait()
        fill_and_place(turn, place, q * each, (q + 1) * each, CELLS // LANES - 1)

    def invert(n):
        share = CELLS * BAND // (LAT * ADVECTION_TOTAL)
        base, value = n * share, n * (slots * share)
        for u in range(share):
            state_of_cell[cells[base + u]] = value + slots * u

    advect(spans, state_of_cell, rates, flags, packed, tiles, *levels, aside=invert)

    def pack(e):
        base = 0
        for at, width in spans_second(count):
            start = slots * (e * count + at)
            parts = [packed[slot_rows(start, h, width, slots), :] for h in range(slots)]
            if is_packed(count, width):
                o_v[e, base : base + half, :] = jnp.concatenate(parts, axis=0).T[:half]
                base += half
            else:
                for h in range(slots):
                    o_v[e, base : base + half, 0:width] = parts[h].T[:half]
                    base += half

    def pack_two(b, carry):
        pack(2 * b)
        pack(2 * b + 1)
        return carry

    some = devices // GROUPS

    def send(q):
        part = pl.ds(q * some, some)
        return pltpu.make_async_copy(o_v.at[part], o_hbm.at[part], sem_out.at[q])

    for q in range(GROUPS):
        lax.fori_loop(q * some // 2, (q + 1) * some // 2, pack_two, 0)
        send(q).start()
    for q in range(GROUPS):
        send(q).wait()


def second_pass(
    cell_of_state, state_of_cell, place, a_hbm, rates, flags, extra, o_hbm, a_v, packed, o_v, tile_a, tile_b, *rest
):
    (sem_in, sem_out), levels = rest[:2], rest[2:]
    tiles = (tile_a, tile_b)
    count = o_v.shape[0]
    devices = a_v.shape[0]
    spans = spans_second(count)
    slots = len(spans)
    half = count // 2
    some = devices // GROUPS

    def fetch(q):
        part = pl.ds(q * some, some)
        return pltpu.make_async_copy(a_hbm.at[part], a_v.at[part], sem_in.at[q])

    for q in range(GROUPS):
        fetch(q).start()

    def unpack(d, slot):
        tile = tiles[slot]
        base = 0
        for h, (_, width) in enumerate(spans):
            if is_packed(count, width):
                both = a_v[d, base : base + half, :]
                tile[slot_rows(0, h, half, slots), :] = both
                tile[slot_rows(slots * half, h, half, slots), :] = pltpu.roll(both, LANES // 2, 1)
                base += half
            else:
                tile[slot_rows(0, h, count, slots), :] = a_v[d, base : base + count, :]
                base += count

    def lay(d, slot):
        scatter_rows(cell_of_state, d * count, tiles[slot], packed, slots, count)

    fetch(0).wait()
    unpack(0, 0)
    for q in range(GROUPS):
        if q + 1 < GROUPS:
            fetch(q + 1).wait()
        fill_and_place(unpack, lay, q * some, (q + 1) * some, devices - 1)
    advect(spans, state_of_cell, rates, flags, packed, tiles, *levels)
    mine = pl.ds(pl.multiple_of(slots * count * place[0], 8), slots * count)
    packed[mine, :] = packed[mine, :] + extra[...]

    def turn(b, carry):
        for i in range(TURNS):
            c = TURNS * b + i
            at_lane = pl.multiple_of(c * LANES, LANES)
            for h, (at, width) in enumerate(spans):
                block = packed[slot_rows(slots * LANES * c, h, LANES, slots), :]
                o_v[at : at + width, pl.ds(at_lane, LANES)] = block.T[:width]
        return carry

    wide = CELLS // GROUPS

    def send(q):
        part = pl.ds(q * wide, wide)
        return pltpu.make_async_copy(o_v.at[:, part], o_hbm.at[:, part], sem_out.at[q])

    each = wide // LANES // TURNS
    for q in range(GROUPS):
        lax.fori_loop(q * each, (q + 1) * each, turn, 0)
        send(q).start()
    for q in range(GROUPS):
        send(q).wait()


def shards(covariance, advective_ratio, flow_heading_flags, cell_of_state, added_uncertainty):
    count = covariance.shape[0]
    devices = lax.axis_size(AXES)
    here = lax.axis_index(AXES)
    smem = pl.BlockSpec(memory_space=pltpu.SMEM)
    vmem = pl.BlockSpec(memory_space=pltpu.VMEM)
    hbm = pl.BlockSpec(memory_space=pl.ANY)
    f32 = jnp.float32
    first, second = len(spans_first(count)), len(spans_second(count))
    sems = pltpu.SemaphoreType.DMA((GROUPS,))

    def pass_scratch(slots, first_shape, last_shape):
        tile = pltpu.VMEM((slots * max(count, LANES), LANES), f32)
        level = pltpu.VMEM((LAT + 2, count, LON), f32)
        packed = pltpu.VMEM((slots * CELLS, LANES), f32)
        return [
            pltpu.VMEM(first_shape, f32),
            packed,
            pltpu.VMEM(last_shape, f32),
            tile,
            tile,
            sems,
            sems,
            level,
            level,
        ]

    def params(mib):
        return pltpu.CompilerParams(vmem_limit_bytes=mib * MIB)

    def cost(us):
        return pl.CostEstimate(flops=us * 10**6, bytes_accessed=us * 3 * 10**6, transcendentals=0)

    own = advective_ratio[0].reshape(ADVECTION_TOTAL * 2, count)
    held = -(-(count + LANES - math.gcd(count, LANES)) // LANES)
    own = lax.dynamic_update_slice(
        jnp.zeros((ADVECTION_TOTAL * 2, held * LANES), f32), own, (0, count * here % LANES)
    )
    own = jnp.transpose(own.reshape(ADVECTION_TOTAL * 2, held, LANES), (1, 0, 2))
    own = jnp.broadcast_to(own[None], (devices,) + own.shape)
    shared = lax.all_to_all(own, AXES, split_axis=0, concat_axis=0, tiled=True)

    cells_first = first * cell_of_state
    shape = (devices, block_rows(count), LANES)
    sent, rates, states_first = pl.pallas_call(
        first_pass,
        out_shape=(
            jax.ShapeDtypeStruct(shape, f32),
            jax.ShapeDtypeStruct((LAT + held, ADVECTION_TOTAL * 2, LON), f32),
            jax.ShapeDtypeStruct((CELLS,), jnp.int32),
        ),
        in_specs=[smem, smem, hbm, vmem, vmem],
        out_specs=(hbm, vmem, smem),
        scratch_shapes=pass_scratch(first, covariance.shape, shape),
        compiler_params=params(60),
        cost_estimate=cost(25),
        name="first_pass",
    )(cells_first, cell_of_state, covariance, shared, flow_heading_flags)
    arrived = lax.all_to_all(sent, AXES, split_axis=0, concat_axis=0, tiled=True)

    row = lax.broadcasted_iota(jnp.int32, (count, second, LANES), 0)
    slot = lax.broadcasted_iota(jnp.int32, (count, second, LANES), 1) * LANES
    slot = slot + lax.broadcasted_iota(jnp.int32, (count, second, LANES), 2)
    extra = jnp.where(row == slot, added_uncertainty[0][:, None, None], 0.0).reshape(second * count, LANES)
    cells_second, states_second = cells_first, states_first
    if first != second:
        cells_second, states_second = second * cell_of_state, states_first // first * second
    return pl.pallas_call(
        second_pass,
        out_shape=jax.ShapeDtypeStruct((count, CELLS), f32),
        in_specs=[smem, smem, smem, hbm, vmem, vmem, vmem],
        out_specs=hbm,
        scratch_shapes=pass_scratch(second, shape, (count, CELLS)),
        compiler_params=params(60),
        cost_estimate=cost(25),
        name="second_pass",
    )(cells_second, states_second, here.reshape(1), arrived, rates, flow_heading_flags, extra)


def solution(mesh):
    in_specs = (
        P(AXES, None),
        P(None, None, None, AXES),
        P(),
        P(),
        P(None, AXES),
    )
    return jax.shard_map(shards, mesh=mesh, in_specs=in_specs, out_specs=P(AXES, None), check_vma=False)
```

```python
import math

import jax
import jax.numpy as jnp
from jax import lax
from jax.experimental import pallas as pl
from jax.experimental.pallas import tpu as pltpu
from jax.sharding import PartitionSpec as P

LAT = 48
LON = 128
ADVECTION_TOTAL = 4
CELLS = LAT * LON
LANES = 128
AXES = ("row", "col")
GROUPS = 8
BATCH = 16
BAND = 16
TURNS = 6
MIB = 2**20


def spans_first(count):
    half = count // 2
    return ((0, half), (half, half))


def spans_second(count):
    return tuple((at, min(LANES, count - at)) for at in range(0, count, LANES))


def is_packed(count, width):
    return 2 * width == LANES and count > width


def block_rows(count):
    return sum(count // 2 if is_packed(count, width) else count for _, width in spans_second(count))


def slot_rows(start, h, total, slots):
    return pl.ds(start + h, total, stride=slots) if slots > 1 else pl.ds(start, total)


def scatter_rows(index, start, source, target, slots, total):
    for u0 in range(0, total, BATCH):
        some = range(u0, min(u0 + BATCH, total))
        rows = [source[slots * u : slots * (u + 1), :] for u in some]
        for u, row in zip(some, rows):
            target[pl.ds(pl.multiple_of(index[start + u], slots), slots), :] = row


def fill_and_place(fill, place, start, stop, last):
    def body(b, carry):
        i = 2 * b
        fill(i + 1, 1)
        place(i, 0)
        fill(jnp.minimum(i + 2, last), 0)
        place(i + 1, 1)
        return carry

    lax.fori_loop(start // 2, stop // 2, body, 0)


def substep(rates, flags, s, source, target, i):
    def spread(row):
        return jnp.broadcast_to(row, (8, LON))

    at_lane = pl.multiple_of(i * LON, LON)
    rate_x = rates[i, 2 * s : 2 * s + 1, :]
    rate_y = rates[i, 2 * s + 1 : 2 * s + 2, :]
    remain = spread(1.0 - rate_x - rate_y)
    lane = lax.broadcasted_iota(jnp.int32, (1, LON), 1)
    west = flags[0, s, 0:1, pl.ds(at_lane, LON)] == 1
    pick_x = spread(jnp.where(west, lane + (LON - 1), lane + 1) & (LON - 1))
    from_south = spread(flags[0, s, 1:2, pl.ds(at_lane, LON)]) == 1
    rate_x, rate_y = spread(rate_x), spread(rate_y)
    for g in range(0, source.shape[1], 8):
        here = source[i + 1, g : g + 8, :]
        side = jnp.take_along_axis(here, pick_x, axis=1)
        y_side = jnp.where(from_south, source[i, g : g + 8, :], source[i + 2, g : g + 8, :])
        target[i + 1, g : g + 8, :] = remain * here + rate_x * side + rate_y * y_side


def advect(spans, state_of_cell, rates, flags, packed, tiles, level_a, level_b):
    slots = len(spans)
    count = level_a.shape[1]

    def enter(b, carry):
        for i in range(TURNS):
            for h, (at, width) in enumerate(spans):
                block = packed[slot_rows(slots * LON * (TURNS * b + i), h, LON, slots), :]
                level_a[TURNS * b + i + 1, at : at + width, :] = block.T[:width]
        return carry

    lax.fori_loop(0, LAT // TURNS, enter, 0)
    for level in (level_a, level_b):
        for edge in (0, LAT + 1):
            level[edge] = jnp.zeros((count, LON), jnp.float32)
    source, target = level_a, level_b
    for s in range(ADVECTION_TOTAL):

        def band(b, carry, s=s, source=source, target=target):
            for i in range(BAND):
                substep(rates, flags, s, source, target, b * BAND + i)
            return carry

        lax.fori_loop(0, LAT // BAND, band, 0)
        source, target = target, source

    def leave(i, slot, final=source):
        for h, (at, width) in enumerate(spans):
            tiles[slot][slot_rows(0, h, LON, slots), 0:width] = final[i + 1, at : at + width, :].T

    def place(i, slot):
        scatter_rows(state_of_cell, i * LON, tiles[slot], packed, slots, LON)

    leave(0, 0)
    fill_and_place(leave, place, 0, LAT, LAT - 1)


def invert(slots):
    unroll = 128

    def kernel(cell_of_state, cells, state_of_cell, scaled):
        scaled[...] = slots * cells[...]

        def body(b, carry):
            base, value = b * unroll, b * (slots * unroll)
            for u in range(unroll):
                state_of_cell[cell_of_state[base + u]] = value + slots * u
            return carry

        lax.fori_loop(0, CELLS // unroll, body, 0)

    return kernel


def gather_rates(shared, rates, count):
    rates[...] = jnp.zeros_like(rates)
    for d in range(shared.shape[0]):
        for t in range(shared.shape[1]):
            lat = d * count // LANES + t
            rates[lat] = rates[lat] + shared[d, t]


def first_pass(
    cell_of_state, state_of_cell, x_hbm, shared, flags, o_hbm, rates, x_v, packed, o_v, tile_a, tile_b, *rest
):
    (sem_in, sem_out), levels = rest[:2], rest[2:]
    tiles = (tile_a, tile_b)
    count = x_v.shape[0]
    devices = o_v.shape[0]
    spans = spans_first(count)
    slots = len(spans)
    half = count // 2
    wide = CELLS // GROUPS

    def fetch(q):
        part = pl.ds(q * wide, wide)
        return pltpu.make_async_copy(x_hbm.at[:, part], x_v.at[:, part], sem_in.at[q])

    for q in range(GROUPS):
        fetch(q).start()
    gather_rates(shared, rates, count)

    def turn(c, slot):
        at_lane = pl.multiple_of(c * LANES, LANES)
        for h, (at, width) in enumerate(spans):
            block = x_v[at : at + width, pl.ds(at_lane, LANES)]
            tiles[slot][slot_rows(0, h, LANES, slots), 0:width] = block.T

    def place(c, slot):
        scatter_rows(cell_of_state, c * LANES, tiles[slot], packed, slots, LANES)

    each = wide // LANES
    fetch(0).wait()
    turn(0, 0)
    for q in range(GROUPS):
        if q + 1 < GROUPS:
            fetch(q + 1).wait()
        fill_and_place(turn, place, q * each, (q + 1) * each, CELLS // LANES - 1)
    advect(spans, state_of_cell, rates, flags, packed, tiles, *levels)

    def pack(e):
        base = 0
        for at, width in spans_second(count):
            start = slots * (e * count + at)
            parts = [packed[slot_rows(start, h, width, slots), :] for h in range(slots)]
            if is_packed(count, width):
                o_v[e, base : base + half, :] = jnp.concatenate(parts, axis=0).T[:half]
                base += half
            else:
                for h in range(slots):
                    o_v[e, base : base + half, 0:width] = parts[h].T[:half]
                    base += half

    def pack_two(b, carry):
        pack(2 * b)
        pack(2 * b + 1)
        return carry

    some = devices // GROUPS

    def send(q):
        part = pl.ds(q * some, some)
        return pltpu.make_async_copy(o_v.at[part], o_hbm.at[part], sem_out.at[q])

    for q in range(GROUPS):
        lax.fori_loop(q * some // 2, (q + 1) * some // 2, pack_two, 0)
        send(q).start()
    for q in range(GROUPS):
        send(q).wait()


def second_pass(
    cell_of_state, state_of_cell, place, a_hbm, rates, flags, extra, o_hbm, a_v, packed, o_v, tile_a, tile_b, *rest
):
    (sem_in, sem_out), levels = rest[:2], rest[2:]
    tiles = (tile_a, tile_b)
    count = o_v.shape[0]
    devices = a_v.shape[0]
    spans = spans_second(count)
    slots = len(spans)
    half = count // 2
    some = devices // GROUPS

    def fetch(q):
        part = pl.ds(q * some, some)
        return pltpu.make_async_copy(a_hbm.at[part], a_v.at[part], sem_in.at[q])

    for q in range(GROUPS):
        fetch(q).start()

    def unpack(d, slot):
        tile = tiles[slot]
        base = 0
        for h, (_, width) in enumerate(spans):
            if is_packed(count, width):
                both = a_v[d, base : base + half, :]
                tile[slot_rows(0, h, half, slots), :] = both
                tile[slot_rows(slots * half, h, half, slots), :] = pltpu.roll(both, LANES // 2, 1)
                base += half
            else:
                tile[slot_rows(0, h, count, slots), :] = a_v[d, base : base + count, :]
                base += count

    def lay(d, slot):
        scatter_rows(cell_of_state, d * count, tiles[slot], packed, slots, count)

    fetch(0).wait()
    unpack(0, 0)
    for q in range(GROUPS):
        if q + 1 < GROUPS:
            fetch(q + 1).wait()
        fill_and_place(unpack, lay, q * some, (q + 1) * some, devices - 1)
    advect(spans, state_of_cell, rates, flags, packed, tiles, *levels)
    mine = pl.ds(pl.multiple_of(slots * count * place[0], 8), slots * count)
    packed[mine, :] = packed[mine, :] + extra[...]

    def turn(b, carry):
        for i in range(TURNS):
            c = TURNS * b + i
            at_lane = pl.multiple_of(c * LANES, LANES)
            for h, (at, width) in enumerate(spans):
                block = packed[slot_rows(slots * LANES * c, h, LANES, slots), :]
                o_v[at : at + width, pl.ds(at_lane, LANES)] = block.T[:width]
        return carry

    wide = CELLS // GROUPS

    def send(q):
        part = pl.ds(q * wide, wide)
        return pltpu.make_async_copy(o_v.at[:, part], o_hbm.at[:, part], sem_out.at[q])

    each = wide // LANES // TURNS
    for q in range(GROUPS):
        lax.fori_loop(q * each, (q + 1) * each, turn, 0)
        send(q).start()
    for q in range(GROUPS):
        send(q).wait()


def shards(covariance, advective_ratio, flow_heading_flags, cell_of_state, added_uncertainty):
    count = covariance.shape[0]
    devices = lax.axis_size(AXES)
    here = lax.axis_index(AXES)
    smem = pl.BlockSpec(memory_space=pltpu.SMEM)
    vmem = pl.BlockSpec(memory_space=pltpu.VMEM)
    hbm = pl.BlockSpec(memory_space=pl.ANY)
    f32 = jnp.float32
    first, second = len(spans_first(count)), len(spans_second(count))
    sems = pltpu.SemaphoreType.DMA((GROUPS,))

    def pass_scratch(slots, first_shape, last_shape):
        tile = pltpu.VMEM((slots * max(count, LANES), LANES), f32)
        level = pltpu.VMEM((LAT + 2, count, LON), f32)
        packed = pltpu.VMEM((slots * CELLS, LANES), f32)
        return [
            pltpu.VMEM(first_shape, f32),
            packed,
            pltpu.VMEM(last_shape, f32),
            tile,
            tile,
            sems,
            sems,
            level,
            level,
        ]

    def params(mib):
        return pltpu.CompilerParams(vmem_limit_bytes=mib * MIB)

    def cost(us):
        return pl.CostEstimate(flops=us * 10**6, bytes_accessed=us * 3 * 10**6, transcendentals=0)

    own = advective_ratio[0].reshape(ADVECTION_TOTAL * 2, count)
    held = -(-(count + LANES - math.gcd(count, LANES)) // LANES)
    own = lax.dynamic_update_slice(
        jnp.zeros((ADVECTION_TOTAL * 2, held * LANES), f32), own, (0, count * here % LANES)
    )
    own = jnp.transpose(own.reshape(ADVECTION_TOTAL * 2, held, LANES), (1, 0, 2))
    own = jnp.broadcast_to(own[None], (devices,) + own.shape)
    shared = lax.all_to_all(own, AXES, split_axis=0, concat_axis=0, tiled=True)

    states_first, cells_first = pl.pallas_call(
        invert(first),
        out_shape=(
            jax.ShapeDtypeStruct((CELLS,), jnp.int32),
            jax.ShapeDtypeStruct((LAT, LON), jnp.int32),
        ),
        in_specs=[smem, vmem],
        out_specs=(smem, vmem),
        cost_estimate=cost(10),
        name="invert",
    )(cell_of_state, cell_of_state.reshape(LAT, LON))
    cells_first = cells_first.reshape(CELLS)

    shape = (devices, block_rows(count), LANES)
    sent, rates = pl.pallas_call(
        first_pass,
        out_shape=(
            jax.ShapeDtypeStruct(shape, f32),
            jax.ShapeDtypeStruct((LAT + held, ADVECTION_TOTAL * 2, LON), f32),
        ),
        in_specs=[smem, smem, hbm, vmem, vmem],
        out_specs=(hbm, vmem),
        scratch_shapes=pass_scratch(first, covariance.shape, shape),
        compiler_params=params(60),
        cost_estimate=cost(25),
        name="first_pass",
    )(cells_first, states_first, covariance, shared, flow_heading_flags)
    arrived = lax.all_to_all(sent, AXES, split_axis=0, concat_axis=0, tiled=True)

    row = lax.broadcasted_iota(jnp.int32, (count, second, LANES), 0)
    slot = lax.broadcasted_iota(jnp.int32, (count, second, LANES), 1) * LANES
    slot = slot + lax.broadcasted_iota(jnp.int32, (count, second, LANES), 2)
    extra = jnp.where(row == slot, added_uncertainty[0][:, None, None], 0.0).reshape(second * count, LANES)
    cells_second, states_second = cells_first, states_first
    if first != second:
        cells_second, states_second = second * cell_of_state, states_first // first * second
    return pl.pallas_call(
        second_pass,
        out_shape=jax.ShapeDtypeStruct((count, CELLS), f32),
        in_specs=[smem, smem, smem, hbm, vmem, vmem, vmem],
        out_specs=hbm,
        scratch_shapes=pass_scratch(second, shape, (count, CELLS)),
        compiler_params=params(60),
        cost_estimate=cost(25),
        name="second_pass",
    )(cells_second, states_second, here.reshape(1), arrived, rates, flow_heading_flags, extra)


def solution(mesh):
    in_specs = (
        P(AXES, None),
        P(None, None, None, AXES),
        P(),
        P(),
        P(None, AXES),
    )
    return jax.shard_map(shards, mesh=mesh, in_specs=in_specs, out_specs=P(AXES, None), check_vma=False)
```
